32 devices in a mesh: wide: 8 (over z, x), narrow: 4 (over y, core).
Axes of the slice: x: 2, y: 2, z: 4, core: 2. Of those that a mesh axis runs over, the one named last changes fastest.
Arguments:
- patches: bfloat16 [16384, 768], P(('wide', 'narrow')), may hold values from -6 to 6
- cotangent: bfloat16 [16384, 768], P(('wide', 'narrow')), may hold values from -6 to 6
- item_len: int32 [8, 4], P('wide'), may hold values from 0 to 2048, as said below
- valid_count: int32 [8, 4], P('wide'), may hold values from 0 to 2048, as said below
- norm1_gain: bfloat16 [768], P('wide'), may hold values from 0.5 to 1.5
- query_weight: bfloat16 [768, 768], P('wide', 'narrow'), may hold values from -0.0546875 to 0.0546875
- key_weight: bfloat16 [768, 768], P('wide', 'narrow'), may hold values from -0.21875 to 0.21875
- value_weight: bfloat16 [768, 768], P('wide', 'narrow'), may hold values from -0.21875 to 0.21875
- out_weight: bfloat16 [768, 768], P('narrow', 'wide'), may hold values from -1.75 to 1.75
- norm2_gain: bfloat16 [768], P('wide'), may hold values from 0.5 to 1.5
- gate_weight: bfloat16 [768, 2048], P('wide', 'narrow'), may hold values from -0.21875 to 0.21875
- up_weight: bfloat16 [768, 2048], P('wide', 'narrow'), may hold values from -0.21875 to 0.21875
- down_weight: bfloat16 [2048, 768], P('narrow', 'wide'), may hold values from -0.25 to 0.25
Outputs:
- output: bfloat16 [16384, 768], P(('wide', 'narrow'))
- grad_input: float32 [16384, 768], P(('wide', 'narrow'))
- grad_norm1: float32 [768], P('wide')
- grad_query: float32 [768, 768], P('wide', 'narrow')
- grad_key: float32 [768, 768], P('wide', 'narrow')
- grad_value: float32 [768, 768], P('wide', 'narrow')
- grad_out: float32 [768, 768], P('narrow', 'wide')
- grad_norm2: float32 [768], P('wide')
- grad_gate: float32 [768, 2048], P('wide', 'narrow')
- grad_up: float32 [768, 2048], P('wide', 'narrow')
- grad_down: float32 [2048, 768], P('narrow', 'wide')
The draws below stay inside these ranges and needn't reach their ends.
Inputs may be any that keep to these rules, and one draw needn't show every extreme that they name: `item_len`: each row sums to 2048; its nonzero entries, each 512, 1024 or 2048, come before its zeros; some row is a single item of 2048. `valid_count`: each entry lies between half the matching item_len (rounded up) and that item_len; 0 for an empty slot; some item is wholly valid.
All inputs are finite; a program needn't handle non-finite values.
Results may differ from the reference program's by a relative error of at most 0.02.
Values may be sent and summed in bfloat16 or wider, within the bound.
No kernel may reach another device: no remote copies, remote signals or barrier semaphores. Data moves between devices by JAX's collectives and lax.ppermute only.
A program may use at most 192 MiB of HBM per device.

```python
import jax
import jax.numpy as jnp
import numpy as np
from jax import lax

D = 768
HEADS = 12
HEAD = 64
FF = 2048
UNIT = 512
ITEMS = 4
BUCKET = 2048
NBUCKETS = 8
TOKENS = 16384


PATTERNS = np.array([[4, 0, 0, 0], [2, 2, 0, 0], [2, 1, 1, 0], [1, 2, 1, 0], [1, 1, 2, 0], [1, 1, 1, 1]], dtype=np.int32)


def item_layout(key):
    pattern = jax.random.randint(jax.random.fold_in(key, 7), (NBUCKETS,), 0, 6)
    pattern = pattern.at[0].set(0)
    lengths = jnp.asarray(PATTERNS)[pattern] * UNIT
    trimmed = jax.random.randint(jax.random.fold_in(key, 11), (NBUCKETS, ITEMS), 0, 1 << 20) % (lengths // 2 + 1)
    counts = lengths - trimmed
    counts = counts.at[0, 0].set(lengths[0, 0])
    return (lengths.astype(jnp.int32), counts.astype(jnp.int32))


def draw_item_len(key, part):
    return item_layout(key)[0]


def draw_valid_count(key, part):
    return item_layout(key)[1]


def strengthened(values, key, source, target, shards_of, factor):
    owner, partner = [(jnp.arange(values.shape[position]) // (values.shape[position] // shards_of)).reshape([-1 if axis == position else 1 for axis in range(values.ndim)]) for position in (source, target)]
    chosen = jax.random.permutation(key, shards_of)[partner]
    strong = (owner == chosen) | (owner == (partner + shards_of // 2) % shards_of)
    return jnp.where(strong, factor * values, values)


def levels(own_key, extent, cuts, low, high):
    loudness = 1.0
    for axis_at, parts in cuts:
        heights = jax.random.uniform(jax.random.fold_in(jax.random.fold_in(own_key, 6), axis_at), (parts,), jnp.float32, low / len(cuts), high / len(cuts))
        loudness = loudness * jnp.repeat(jnp.exp(heights), extent[axis_at] // parts).reshape((-1,) + (1,) * (len(extent) - 1 - axis_at))
    return loudness


def noise(stream_key, extent, deviation, bound, cuts=(), kind=jnp.bfloat16):
    loudness = levels(stream_key, extent, cuts, -0.22, 0.18) if cuts else 1.0
    entries = jax.random.normal(stream_key, extent, jnp.float32) * deviation * loudness
    return jnp.minimum(jnp.maximum(entries, -bound), bound).astype(kind)


def bell_draw_with(own_key, dims, deviation, limit, shards, heavy, kind=jnp.bfloat16):
    values = deviation * jax.random.normal(own_key, dims, jnp.float32)
    if shards:
        values = values * levels(own_key, dims, shards, -0.22, 0.18)
    return jnp.clip(strengthened(values, jax.random.fold_in(own_key, 3), *heavy), -limit, limit).astype(kind)


def setup_inputs(seed: int = 0) -> dict:
    streams_of = jax.random.split(jax.random.key(seed), 14)
    patches = bell_draw_with(streams_of[0], (TOKENS, D), 1.0, 6.0, ((0, 32),), (0, 1, 32, 2.75))
    cotangent = bell_draw_with(streams_of[1], (TOKENS, D), 1.0, 6.0, ((0, 32),), (0, 1, 32, 2.75))
    item_len = draw_item_len(jax.random.fold_in(streams_of[13], 71), 0)
    valid_count = draw_valid_count(jax.random.fold_in(streams_of[13], 71), 0)
    norm1_gain = jnp.clip(1.0 + 0.1 * jax.random.normal(streams_of[4], (D,), jnp.float32), 0.5, 1.5).astype(jnp.bfloat16)
    query_weight = noise(streams_of[5], (D, HEADS * HEAD), (16 * D) ** -0.5, 0.0546875, ((0, 8), (1, 4)))
    key_weight = noise(streams_of[6], (D, HEADS * HEAD), D ** -0.5, 0.21875, ((0, 8), (1, 4)))
    value_weight = noise(streams_of[7], (D, HEADS * HEAD), D ** -0.5, 0.21875, ((0, 8), (1, 4)))
    out_weight = noise(streams_of[8], (HEADS * HEAD, D), (HEADS * HEAD // 64) ** -0.5, 1.75, ((0, 4), (1, 8)))
    norm2_gain = jnp.clip(1.0 + 0.1 * jax.random.normal(streams_of[9], (D,), jnp.float32), 0.5, 1.5).astype(jnp.bfloat16)
    gate_weight = noise(streams_of[10], (D, FF), D ** -0.5, 0.21875, ((0, 8), (1, 4)))
    up_weight = noise(streams_of[11], (D, FF), D ** -0.5, 0.21875, ((0, 8), (1, 4)))
    down_weight = noise(streams_of[12], (FF, D), (FF // 4) ** -0.5, 0.25, ((0, 4), (1, 8)))
    return {"patches": patches, "cotangent": cotangent, "item_len": item_len, "valid_count": valid_count, "norm1_gain": norm1_gain, "query_weight": query_weight, "key_weight": key_weight, "value_weight": value_weight, "out_weight": out_weight, "norm2_gain": norm2_gain, "gate_weight": gate_weight, "up_weight": up_weight, "down_weight": down_weight}


EPSILON = 1e-06
MASKED = -1e+30

@jax.custom_vjp
def low(v):
    return lax.optimization_barrier(v.astype(jnp.bfloat16)).astype(jnp.float32)

@jax.custom_vjp
def low_back(v):
    return v

def low_keep(v):
    return (low(v), None)

def low_pass(kept, grad):
    return (grad,)

def back_keep(v):
    return (v, None)

def back_low(kept, grad):
    return (low(grad),)
low.defvjp(low_keep, low_pass)
low_back.defvjp(back_keep, back_low)

def normalize(values, gain):
    return values * lax.rsqrt(lax.optimization_barrier(jnp.mean(values * values, axis=-1, keepdims=True)) + EPSILON) * gain

def matmul(left, right):
    return jnp.dot(left, right, precision=lax.Precision.HIGHEST)

def key_mask(lengths, counts):
    places = jnp.arange(BUCKET, dtype=jnp.int32)
    starts = (jnp.cumsum(lengths) - lengths).astype(jnp.int32)
    inside = (places[:, None] >= starts[None, :]) & (places[:, None] < (starts + lengths)[None, :])
    slot_ids = jnp.arange(lengths.shape[0], dtype=jnp.int32)
    item_of = lax.optimization_barrier(jnp.sum(jnp.where(inside, slot_ids[None, :], 0), axis=1)).astype(jnp.int32)
    valid_end = lax.optimization_barrier(jnp.sum(jnp.where(inside, (starts + counts)[None, :], 0), axis=1)).astype(jnp.int32)
    return (item_of[:, None] == item_of[None, :]) & (places[None, :] < valid_end[None, :])

def attend_bucket(pieces):
    bucket_query, bucket_key, bucket_value, bucket_len, bucket_count = pieces
    allowed = key_mask(bucket_len, bucket_count)
    scores = low_back(jnp.einsum('qhe,khe->hqk', bucket_query, bucket_key, precision=lax.Precision.HIGHEST))
    scores = jnp.where(allowed[None], scores, MASKED)
    probs = low(jax.nn.softmax(scores, axis=-1))
    return jnp.einsum('hqk,khe->qhe', probs, bucket_value, precision=lax.Precision.HIGHEST)

def reference(patches, cotangent, item_len, valid_count, norm1_gain, query_weight, key_weight, value_weight, out_weight, norm2_gain, gate_weight, up_weight, down_weight):
    floats = tuple((a.astype(jnp.float32) for a in (patches, norm1_gain, query_weight, key_weight, value_weight, out_weight, norm2_gain, gate_weight, up_weight, down_weight)))

    def forward(inputs, gain_one, query_w, key_w, value_w, out_w, gain_two, gate_w, up_w, down_w):
        normed_one = low(normalize(inputs, gain_one))
        queries = low(low_back(matmul(normed_one, query_w)))
        keys_all = low(low_back(matmul(normed_one, key_w)))
        values_all = low(low_back(matmul(normed_one, value_w)))
        bucket_shape = (NBUCKETS, BUCKET, HEADS, HEAD)
        attended = lax.map(jax.checkpoint(attend_bucket), (queries.reshape(bucket_shape), keys_all.reshape(bucket_shape), values_all.reshape(bucket_shape), item_len, valid_count))
        attended = low(low_back(attended.reshape(TOKENS, HEADS * HEAD)))
        middle = inputs + low_back(matmul(attended, out_w))
        normed_two = low(normalize(middle, gain_two))
        gate_act = low_back(matmul(normed_two, gate_w))
        up_act = low_back(matmul(normed_two, up_w))
        hidden = low(jax.nn.gelu(gate_act, approximate=True) * up_act)
        return middle + low_back(matmul(hidden, down_w))
    result, pullback = jax.vjp(forward, *floats)
    gradients = pullback(cotangent.astype(jnp.float32))
    return (result.astype(jnp.bfloat16), gradients[0], gradients[1], gradients[2], gradients[3], gradients[4], gradients[5], gradients[6], gradients[7], gradients[8], gradients[9])
```

```python
import functools

import jax
import jax.numpy as jnp
from jax import lax
from jax.experimental import pallas as pl
from jax.experimental.pallas import tpu as pltpu
from jax.sharding import PartitionSpec as P

HEAD = 64
BUCKET = 2048
EPSILON = 1e-06
MASKED = -1e30
NARROW = 4


NT = (((1,), (1,)), ((), ()))
NN = (((1,), (0,)), ((), ()))
TN = (((0,), (0,)), ((), ()))


def dot(left, right, dims=NN):
    return lax.dot_general(left, right, dims, preferred_element_type=jnp.float32)


def low(values):
    return values.astype(jnp.bfloat16)


def wide32(values):
    return values.astype(jnp.float32)


def swap(values, axis, bits):
    size = lax.axis_size(axis)
    return lax.ppermute(values, axis, [(i, i ^ bits) for i in range(size)])


def gather_rows(own):
    across = swap(own, "narrow", 2)
    return jnp.concatenate([own, swap(own, "narrow", 1), across, swap(across, "narrow", 1)], axis=0)


def reduce_rows(partial):
    rows = partial.shape[0] // NARROW
    part = [low(partial[j * rows : (j + 1) * rows]) for j in range(NARROW)]
    far = wide32(part[2]) + wide32(swap(part[3], "narrow", 1))
    near = wide32(part[0]) + wide32(swap(part[1], "narrow", 1))
    return near + wide32(swap(low(far), "narrow", 2))


def gather_wide(own):
    size = lax.axis_size("wide")
    if size != 8:
        return lax.all_gather(own, "wide", axis=0, tiled=True)
    rows, cols = own.shape
    index = lax.axis_index("wide")
    z, x = index // 2, index % 2
    column = jnp.zeros((4, rows, cols), own.dtype)
    column = lax.dynamic_update_slice(column, own[None], (z, 0, 0))
    for k in (1, 2, 3):
        column = lax.dynamic_update_slice(column, swap(own, "wide", 2 * k)[None], (z ^ k, 0, 0))
    other = swap(column, "wide", 1)
    first = jnp.where(x == 0, column, other)
    second = jnp.where(x == 0, other, column)
    return jnp.stack([first, second], axis=1).reshape(size * rows, cols)


def reduce_wide(partial):
    size = lax.axis_size("wide")
    rows, cols = partial.shape[0] // size, partial.shape[1]
    if size != 8:
        pieces = lax.all_to_all(low(partial).reshape(size, rows, cols), "wide", 0, 0, tiled=True)
        return jnp.sum(wide32(pieces), axis=0)
    index = lax.axis_index("wide")
    z, x = index // 2, index % 2
    blocks = low(partial).reshape(4, 2, rows, cols)
    mine = jnp.where(x == 0, blocks[:, 0], blocks[:, 1])
    theirs = jnp.where(x == 0, blocks[:, 1], blocks[:, 0])
    column = low(wide32(mine) + wide32(swap(theirs, "wide", 1)))
    total = wide32(lax.dynamic_index_in_dim(column, z, 0, keepdims=False))
    for k in (1, 2, 3):
        piece = lax.dynamic_index_in_dim(column, z ^ k, 0, keepdims=False)
        total = total + wide32(swap(piece, "wide", 2 * k))
    return total


def sum_narrow(values):
    values = values + swap(values, "narrow", 1)
    return values + swap(values, "narrow", 2)


def key_bias(len_ref, cnt_ref, own_ref, row, items):
    unit = BUCKET // NARROW
    own = own_ref[0]
    col = lax.broadcasted_iota(jnp.int32, (1, BUCKET), 1)
    col = ((col // unit) ^ own) * unit + col % unit
    row = ((row // unit) ^ own) * unit
    start = jnp.int32(0)
    low_end = jnp.int32(0)
    high_end = jnp.int32(0)
    for i in range(items):
        length = len_ref[0, i]
        inside = (row >= start) & (row < start + length)
        low_end = jnp.where(inside, start, low_end)
        high_end = jnp.where(inside, start + cnt_ref[0, i], high_end)
        start = start + length
    return jnp.where((col >= low_end) & (col < high_end), 0.0, MASKED).astype(jnp.float32)


def forward_kernel(len_ref, cnt_ref, own_ref, q_ref, k_ref, v_ref, o_ref, lse_ref, *, block, heads, items):
    bias = key_bias(len_ref, cnt_ref, own_ref, pl.program_id(0) * block, items)
    for h in range(heads):
        cols = slice(h * HEAD, (h + 1) * HEAD)
        scores = dot(q_ref[:, cols], k_ref[:, cols], NT) + bias
        highest = jnp.max(scores, axis=-1, keepdims=True)
        weights = jnp.exp(scores - highest)
        total = jnp.sum(weights, axis=-1, keepdims=True)
        o_ref[:, cols] = low(dot(low(weights), v_ref[:, cols]) / total)
        lse_ref[:, h : h + 1] = highest + jnp.log(total)


def attention_forward(scalars, q, k, v, block=256):
    tokens, width = q.shape
    heads, items = width // HEAD, scalars[0].shape[1]
    row = pl.BlockSpec((block, width), lambda i, *_: (i, 0))
    full = pl.BlockSpec((tokens, width), lambda i, *_: (0, 0))
    return pl.pallas_call(
        functools.partial(forward_kernel, block=block, heads=heads, items=items),
        out_shape=(
            jax.ShapeDtypeStruct((tokens, width), jnp.bfloat16),
            jax.ShapeDtypeStruct((tokens, heads), jnp.float32),
        ),
        grid_spec=pltpu.PrefetchScalarGridSpec(
            num_scalar_prefetch=3,
            grid=(tokens // block,),
            in_specs=[row, full, full],
            out_specs=[row, pl.BlockSpec((block, heads), lambda i, *_: (i, 0))],
        ),
        compiler_params=pltpu.CompilerParams(
            dimension_semantics=("arbitrary",), vmem_limit_bytes=48 << 20
        ),
        name="attention_forward",
    )(*scalars, q, k, v)


def backward_kernel(
    len_ref, cnt_ref, own_ref, q_ref, k_ref, v_ref, do_ref, o_ref, lse_ref,
    dq_ref, dk_ref, dv_ref, dk_sum, dv_sum, *, block, heads, items
):
    step = pl.program_id(0)
    bias = key_bias(len_ref, cnt_ref, own_ref, step * block, items)

    @pl.when(step == 0)
    def _():
        dk_sum[...] = jnp.zeros_like(dk_sum)
        dv_sum[...] = jnp.zeros_like(dv_sum)

    for h in range(heads):
        cols = slice(h * HEAD, (h + 1) * HEAD)
        q, k, v, do = q_ref[:, cols], k_ref[:, cols], v_ref[:, cols], do_ref[:, cols]
        delta = jnp.sum(wide32(do) * wide32(o_ref[:, cols]), axis=-1, keepdims=True)
        probs = jnp.exp(dot(q, k, NT) + bias - lse_ref[:, h : h + 1])
        ds = low(probs * (dot(do, v, NT) - delta))
        dq_ref[:, cols] = low(dot(ds, k))
        dv_sum[cols, :] += dot(do, low(probs), TN)
        dk_sum[cols, :] += dot(q, ds, TN)

    @pl.when(step == pl.num_programs(0) - 1)
    def _():
        dk_ref[...] = low(dk_sum[...].T)
        dv_ref[...] = low(dv_sum[...].T)


def attention_backward(scalars, q, k, v, do, o, lse, block=256):
    tokens, width = q.shape
    heads, items = width // HEAD, scalars[0].shape[1]
    row = pl.BlockSpec((block, width), lambda i, *_: (i, 0))
    full = pl.BlockSpec((tokens, width), lambda i, *_: (0, 0))
    return pl.pallas_call(
        functools.partial(backward_kernel, block=block, heads=heads, items=items),
        out_shape=(jax.ShapeDtypeStruct((tokens, width), jnp.bfloat16),) * 3,
        grid_spec=pltpu.PrefetchScalarGridSpec(
            num_scalar_prefetch=3,
            grid=(tokens // block,),
            in_specs=[row, full, full, row, row, pl.BlockSpec((block, heads), lambda i, *_: (i, 0))],
            out_specs=[row, full, full],
            scratch_shapes=[pltpu.VMEM((width, tokens), jnp.float32)] * 2,
        ),
        compiler_params=pltpu.CompilerParams(
            dimension_semantics=("arbitrary",), vmem_limit_bytes=48 << 20
        ),
        name="attention_backward",
    )(*scalars, q, k, v, do, o, lse)


def inverse_rms(values):
    return lax.rsqrt(jnp.mean(values * values, axis=-1, keepdims=True) + EPSILON)


def norm_back(values, gain, grad):
    r = inverse_rms(values)
    n = values * r
    scaled = gain * grad
    return r * (scaled - n * jnp.mean(scaled * n, axis=-1, keepdims=True))


def gated(gate_in, up_in):
    return jax.nn.gelu(gate_in, approximate=True) * up_in


def on_device(
    patches, cotangent, item_len, valid_count, norm1_gain, query_weight, key_weight, value_weight,
    out_weight, norm2_gain, gate_weight, up_weight, down_weight,
):
    width = query_weight.shape[1]
    hidden_dev = gate_weight.shape[1]
    rows_dev = query_weight.shape[0]
    scalars = (item_len, valid_count, lax.axis_index("narrow").astype(jnp.int32).reshape(1))
    gains = jnp.pad(jnp.stack([norm1_gain, norm2_gain], axis=1), ((0, 0), (0, 126)))
    attn_w = gather_wide(
        jnp.concatenate([query_weight, key_weight, value_weight, out_weight.T, gains], axis=1)
    )
    rows = gather_rows(patches)
    mlp_w = gather_wide(jnp.concatenate([gate_weight, up_weight, down_weight.T], axis=1))
    cot = gather_rows(cotangent)
    qkv_w = attn_w[:, : 3 * width]
    out_w = attn_w[:, 3 * width : 4 * width]
    gain_one = wide32(attn_w[:, 4 * width])
    gain_two = wide32(attn_w[:, 4 * width + 1])
    gate_w, up_w = mlp_w[:, :hidden_dev], mlp_w[:, hidden_dev : 2 * hidden_dev]
    down_w = mlp_w[:, 2 * hidden_dev :]

    x = wide32(rows)
    n_one = x * inverse_rms(x)
    h_one = low(n_one * gain_one)
    qkv = low(dot(h_one, qkv_w))
    q, k, v = qkv[:, :width], qkv[:, width : 2 * width], qkv[:, 2 * width :]
    o, lse = attention_forward(scalars, q, k, v)
    middle_own = wide32(patches) + reduce_rows(dot(o, out_w, NT))
    middle = wide32(gather_rows(low(middle_own)))
    n_two = middle * inverse_rms(middle)
    h_two = low(n_two * gain_two)
    gate_act = dot(h_two, gate_w)
    up_act = dot(h_two, up_w)
    hidden = low(gated(gate_act, up_act))
    output = low(middle_own + reduce_rows(dot(hidden, down_w, NT)))

    grad_hidden = dot(cot, down_w)
    _, pullback = jax.vjp(gated, gate_act, up_act)
    grad_gate_act, grad_up_act = (low(a) for a in pullback(grad_hidden))
    dh_two = dot(grad_gate_act, gate_w, NT) + dot(grad_up_act, up_w, NT)
    norm_two_part = jnp.sum(dh_two * n_two, axis=0)
    middle_grad_own = wide32(cotangent) + norm_back(middle_own, gain_two, reduce_rows(dh_two))
    middle_grad = gather_rows(low(middle_grad_own))
    mlp_sums = reduce_wide(
        jnp.concatenate(
            [dot(h_two, grad_gate_act, TN), dot(h_two, grad_up_act, TN), dot(cot, hidden, TN)], axis=1
        )
    )
    do = low(dot(middle_grad, out_w))
    dq, dk, dv = attention_backward(scalars, q, k, v, do, o, lse)
    dqkv = jnp.concatenate([dq, dk, dv], axis=1)
    dh_one = dot(dqkv, qkv_w, NT)
    norm_one_part = jnp.sum(dh_one * n_one, axis=0)
    grad_input = middle_grad_own + norm_back(
        wide32(patches), gain_one, reduce_rows(dh_one)
    )
    norms = sum_narrow(jnp.stack([norm_one_part, norm_two_part], axis=1))
    attn_sums = reduce_wide(
        jnp.concatenate(
            [dot(h_one, dqkv, TN), dot(middle_grad, o, TN), jnp.pad(norms, ((0, 0), (0, 126)))], axis=1
        )
    )
    return (
        output,
        grad_input,
        attn_sums[:, 4 * width],
        attn_sums[:, :width],
        attn_sums[:, width : 2 * width],
        attn_sums[:, 2 * width : 3 * width],
        attn_sums[:, 3 * width : 4 * width].T,
        attn_sums[:, 4 * width + 1],
        mlp_sums[:, :hidden_dev],
        mlp_sums[:, hidden_dev : 2 * hidden_dev],
        mlp_sums[:, 2 * hidden_dev :].T,
    )


def solution(mesh):
    tokens = P(("wide", "narrow"), None)
    return jax.shard_map(
        on_device,
        mesh=mesh,
        in_specs=(
            tokens, tokens, P("wide", None), P("wide", None), P("wide"), P("wide", "narrow"),
            P("wide", "narrow"), P("wide", "narrow"), P("narrow", "wide"), P("wide"),
            P("wide", "narrow"), P("wide", "narrow"), P("narrow", "wide"),
        ),
        out_specs=(
            tokens, tokens, P("wide"), P("wide", "narrow"), P("wide", "narrow"), P("wide", "narrow"),
            P("narrow", "wide"), P("wide"), P("wide", "narrow"), P("wide", "narrow"), P("narrow", "wide"),
        ),
        check_vma=False,
    )
```

```python
import functools

import jax
import jax.numpy as jnp
from jax import lax
from jax.experimental import pallas as pl
from jax.experimental.pallas import tpu as pltpu
from jax.sharding import PartitionSpec as P

HEAD = 64
BUCKET = 2048
EPSILON = 1e-06
MASKED = -1e30
NARROW = 4


NT = (((1,), (1,)), ((), ()))
NN = (((1,), (0,)), ((), ()))
TN = (((0,), (0,)), ((), ()))


def dot(left, right, dims=NN):
    return lax.dot_general(left, right, dims, preferred_element_type=jnp.float32)


def low(values):
    return values.astype(jnp.bfloat16)


def wide32(values):
    return values.astype(jnp.float32)


def swap(values, axis, bits):
    size = lax.axis_size(axis)
    return lax.ppermute(values, axis, [(i, i ^ bits) for i in range(size)])


def gather_halves(own):
    across = swap(own, "narrow", 2)
    near = jnp.concatenate([own, swap(own, "narrow", 1)], axis=0)
    far = jnp.concatenate([across, swap(across, "narrow", 1)], axis=0)
    return near, far


def pair_sum(half):
    rows = half.shape[0] // 2
    return wide32(half[:rows]) + wide32(swap(half[rows:], "narrow", 1))


def cross(values):
    return wide32(swap(low(values), "narrow", 2))


def gather_wide(own):
    size = lax.axis_size("wide")
    if size != 8:
        return lax.all_gather(own, "wide", axis=0, tiled=True)
    rows, cols = own.shape
    index = lax.axis_index("wide")
    z, x = index // 2, index % 2
    column = jnp.zeros((4, rows, cols), own.dtype)
    column = lax.dynamic_update_slice(column, own[None], (z, 0, 0))
    for k in (1, 2, 3):
        column = lax.dynamic_update_slice(column, swap(own, "wide", 2 * k)[None], (z ^ k, 0, 0))
    other = swap(column, "wide", 1)
    first = jnp.where(x == 0, column, other)
    second = jnp.where(x == 0, other, column)
    return jnp.stack([first, second], axis=1).reshape(size * rows, cols)


def reduce_wide(partial):
    size = lax.axis_size("wide")
    rows, cols = partial.shape[0] // size, partial.shape[1]
    if size != 8:
        pieces = lax.all_to_all(low(partial).reshape(size, rows, cols), "wide", 0, 0, tiled=True)
        return jnp.sum(wide32(pieces), axis=0)
    index = lax.axis_index("wide")
    z, x = index // 2, index % 2
    blocks = low(partial).reshape(4, 2, rows, cols)
    mine = jnp.where(x == 0, blocks[:, 0], blocks[:, 1])
    theirs = jnp.where(x == 0, blocks[:, 1], blocks[:, 0])
    column = low(wide32(mine) + wide32(swap(theirs, "wide", 1)))
    total = wide32(lax.dynamic_index_in_dim(column, z, 0, keepdims=False))
    for k in (1, 2, 3):
        piece = lax.dynamic_index_in_dim(column, z ^ k, 0, keepdims=False)
        total = total + wide32(swap(piece, "wide", 2 * k))
    return total


def sum_narrow(values):
    values = values + swap(values, "narrow", 1)
    return values + swap(values, "narrow", 2)


def call(kernel, name, grid, in_specs, out_specs, out_shape, scratch=(), prefetch=0):
    return pl.pallas_call(
        kernel,
        out_shape=out_shape,
        grid_spec=pltpu.PrefetchScalarGridSpec(
            num_scalar_prefetch=prefetch,
            grid=grid,
            in_specs=in_specs,
            out_specs=out_specs,
            scratch_shapes=scratch,
        ),
        compiler_params=pltpu.CompilerParams(
            dimension_semantics=("arbitrary",) * len(grid), vmem_limit_bytes=52 << 20
        ),
        name=name,
    )


def by_row(block, width):
    return pl.BlockSpec((block, width), lambda i, *_: (i, 0))


def whole(*shape):
    return pl.BlockSpec(shape, lambda i, *_: (0,) * len(shape))


def shaped(shape, dtype=jnp.bfloat16):
    return jax.ShapeDtypeStruct(shape, dtype)


def inverse_rms(values):
    return lax.rsqrt(jnp.mean(values * values, axis=-1, keepdims=True) + EPSILON)


def eight(values):
    return jnp.sum(values.reshape(values.shape[0] // 8, 8, values.shape[1]), axis=0)


def project_kernel(x_ref, gain_ref, w_ref, h_ref, q_ref, k_ref, v_ref, *, width):
    x = wide32(x_ref[...])
    h = low(x * inverse_rms(x) * gain_ref[...])
    h_ref[...] = h
    qkv = low(dot(h, w_ref[...]))
    q_ref[...] = qkv[:, :width]
    k_ref[...] = qkv[:, width : 2 * width]
    v_ref[...] = qkv[:, 2 * width :]


def project(rows, gain, weight, block=512):
    tokens, d = rows.shape
    width = weight.shape[1] // 3
    return call(
        functools.partial(project_kernel, width=width),
        "project",
        (tokens // block,),
        [by_row(block, d), whole(1, d), whole(d, 3 * width)],
        [by_row(block, d)] + [by_row(block, width)] * 3,
        [shaped((tokens, d))] + [shaped((tokens, width))] * 3,
    )(rows, gain, weight)


def key_bias(len_ref, cnt_ref, own_ref, row, items):
    unit = BUCKET // NARROW
    own = own_ref[0]
    col = lax.broadcasted_iota(jnp.int32, (1, BUCKET), 1)
    col = ((col // unit) ^ own) * unit + col % unit
    row = ((row // unit) ^ own) * unit
    start = jnp.int32(0)
    low_end = jnp.int32(0)
    high_end = jnp.int32(0)
    for i in range(items):
        length = len_ref[0, i]
        inside = (row >= start) & (row < start + length)
        low_end = jnp.where(inside, start, low_end)
        high_end = jnp.where(inside, start + cnt_ref[0, i], high_end)
        start = start + length
    return jnp.where((col >= low_end) & (col < high_end), 0.0, MASKED).astype(jnp.float32)


def forward_kernel(
    len_ref, cnt_ref, own_ref, q_ref, k_ref, v_ref, w_ref, o_ref, lse_ref, part_ref, *, first, block, heads, items
):
    bias = key_bias(len_ref, cnt_ref, own_ref, first + pl.program_id(0) * block, items)
    for h in range(heads):
        cols = slice(h * HEAD, (h + 1) * HEAD)
        scores = dot(q_ref[:, cols], k_ref[:, cols], NT) + bias
        highest = jnp.max(scores, axis=-1, keepdims=True)
        weights = jnp.exp(scores - highest)
        total = jnp.sum(weights, axis=-1, keepdims=True)
        o_ref[:, cols] = low(dot(low(weights), v_ref[:, cols]) / total)
        lse_ref[:, h : h + 1] = highest + jnp.log(total)
    part_ref[...] = low(dot(o_ref[...], w_ref[...], NT))


def attention_forward(scalars, q, k, v, out_w, first, block=256):
    tokens, width = q.shape
    heads, items, d = width // HEAD, scalars[0].shape[1], out_w.shape[0]
    rows = tokens // 2
    at = first // block
    row = pl.BlockSpec((block, width), lambda i, *_: (i + at, 0))
    return call(
        functools.partial(forward_kernel, first=first, block=block, heads=heads, items=items),
        "attention_forward",
        (rows // block,),
        [row, whole(tokens, width), whole(tokens, width), whole(d, width)],
        [by_row(block, width), by_row(block, heads), by_row(block, d)],
        [shaped((rows, width)), shaped((rows, heads), jnp.float32), shaped((rows, d))],
        prefetch=3,
    )(*scalars, q, k, v, out_w)


def backward_kernel(
    len_ref, cnt_ref, own_ref, q_ref, k_ref, v_ref, g_ref, w_ref, o_ref, lse_ref, *rest, first, block, heads, items
):
    if first:
        dk_in, dv_in, dq_ref, dk_ref, dv_ref, dk_sum, dv_sum = rest
    else:
        dq_ref, dk_sum, dv_sum = rest
    step = pl.program_id(0)
    bias = key_bias(len_ref, cnt_ref, own_ref, first + step * block, items)

    @pl.when(step == 0)
    def _():
        dk_sum[...] = dk_in[...] if first else jnp.zeros_like(dk_sum)
        dv_sum[...] = dv_in[...] if first else jnp.zeros_like(dv_sum)

    do_all = low(dot(g_ref[...], w_ref[...]))
    for h in range(heads):
        cols = slice(h * HEAD, (h + 1) * HEAD)
        q, k, v, do = q_ref[:, cols], k_ref[:, cols], v_ref[:, cols], do_all[:, cols]
        delta = jnp.sum(wide32(do) * wide32(o_ref[:, cols]), axis=-1, keepdims=True)
        probs = jnp.exp(dot(q, k, NT) + bias - lse_ref[:, h : h + 1])
        ds = low(probs * (dot(do, v, NT) - delta))
        dq_ref[:, cols] = low(dot(ds, k))
        dv_sum[cols, :] += dot(do, low(probs), TN)
        dk_sum[cols, :] += dot(q, ds, TN)

    if first:

        @pl.when(step == pl.num_programs(0) - 1)
        def _():
            dk_ref[...] = low(dk_sum[...].T)
            dv_ref[...] = low(dv_sum[...].T)


def attention_backward(scalars, q, k, v, grad, out_w, o, lse, sums, block=256):
    tokens, width = q.shape
    heads, items, d = width // HEAD, scalars[0].shape[1], out_w.shape[0]
    rows = tokens // 2
    first = rows if sums else 0
    at = first // block
    row = pl.BlockSpec((block, width), lambda i, *_: (i + at, 0))
    full = whole(tokens, width)
    turned = whole(width, tokens)
    kept = shaped((width, tokens), jnp.float32)
    in_specs = [row, full, full, by_row(block, d), whole(d, width), by_row(block, width), by_row(block, heads)]
    return call(
        functools.partial(backward_kernel, first=first, block=block, heads=heads, items=items),
        "attention_backward",
        (rows // block,),
        in_specs + ([turned, turned] if sums else []),
        [by_row(block, width)] + ([full, full] if sums else [turned, turned]),
        [shaped((rows, width))] + ([shaped((tokens, width))] * 2 if sums else [kept, kept]),
        scratch=[pltpu.VMEM((width, tokens), jnp.float32)] * 2 if sums else [],
        prefetch=3,
    )(*scalars, q, k, v, grad, out_w, o, lse, *sums)


def mlp_kernel(
    m_ref, g_ref, gain_ref, w_ref, y_ref, dh_ref, h_ref, hid_ref, dg_ref, du_ref, norm_ref, *, width
):
    m = wide32(m_ref[...])
    n = m * inverse_rms(m)
    h = low(n * gain_ref[...])
    h_ref[...] = h
    both = dot(h, w_ref[:, : 2 * width])
    gate, up = both[:, :width], both[:, width:]
    square = gate * gate
    scale = 0.7978845608028654
    t = jnp.tanh(scale * gate * (1.0 + 0.044715 * square))
    half = 0.5 * (1.0 + t)
    act = gate * half
    slope = half + (0.5 * scale) * gate * (1.0 - t * t) * (1.0 + 0.134145 * square)
    hid = low(act * up)
    hid_ref[...] = hid
    y_ref[...] = low(dot(hid, w_ref[:, 2 * width :], NT))
    dhid = dot(g_ref[...], w_ref[:, 2 * width :])
    dgate = low(dhid * up * slope)
    dup = low(dhid * act)
    dg_ref[...] = dgate
    du_ref[...] = dup
    dh = dot(dgate, w_ref[:, :width], NT) + dot(dup, w_ref[:, width : 2 * width], NT)
    dh_ref[...] = low(dh)

    @pl.when(pl.program_id(0) == 0)
    def _():
        norm_ref[...] = jnp.zeros_like(norm_ref)

    norm_ref[...] += eight(dh * n)


def mlp(middle, grad, gain, weight, block=256):
    rows, d = middle.shape
    width = weight.shape[1] // 3
    wide_row, thin_row = by_row(block, d), by_row(block, width)
    return call(
        functools.partial(mlp_kernel, width=width),
        "mlp",
        (rows // block,),
        [wide_row, wide_row, whole(1, d), whole(d, 3 * width)],
        [wide_row] * 3 + [thin_row] * 3 + [whole(8, d)],
        [shaped((rows, d))] * 3 + [shaped((rows, width))] * 3 + [shaped((8, d), jnp.float32)],
    )(middle, grad, gain, weight)


def rows_kernel(dq_ref, dk_ref, dv_ref, x_ref, w_ref, dh_ref, norm_ref, *, width):
    dh = dot(dq_ref[...], w_ref[:, :width], NT)
    dh += dot(dk_ref[...], w_ref[:, width : 2 * width], NT)
    dh += dot(dv_ref[...], w_ref[:, 2 * width :], NT)
    dh_ref[...] = low(dh)
    x = wide32(x_ref[...])

    @pl.when(pl.program_id(0) == 0)
    def _():
        norm_ref[...] = jnp.zeros_like(norm_ref)

    norm_ref[...] += eight(dh * x * inverse_rms(x))


def rows_back(dq, dk, dv, rows, weight, first, block=512):
    count, width = dq.shape
    d = rows.shape[1]
    at = first // block
    return call(
        functools.partial(rows_kernel, width=width),
        "rows_back",
        (count // block,),
        [
            by_row(block, width),
            pl.BlockSpec((block, width), lambda i, *_: (i + at, 0)),
            pl.BlockSpec((block, width), lambda i, *_: (i + at, 0)),
            by_row(block, d),
            whole(d, 3 * width),
        ],
        [by_row(block, d), whole(8, d)],
        [shaped((count, d)), shaped((8, d), jnp.float32)],
    )(dq, dk, dv, rows, weight)


def norm_back(values, gain, grad):
    r = inverse_rms(values)
    n = values * r
    scaled = gain * grad
    return r * (scaled - n * jnp.mean(scaled * n, axis=-1, keepdims=True))


def on_device(
    patches, cotangent, item_len, valid_count, norm1_gain, query_weight, key_weight, value_weight,
    out_weight, norm2_gain, gate_weight, up_weight, down_weight,
):
    width = query_weight.shape[1]
    hidden_dev = gate_weight.shape[1]
    scalars = (item_len, valid_count, lax.axis_index("narrow").astype(jnp.int32).reshape(1))
    gains = jnp.pad(jnp.stack([norm1_gain, norm2_gain], axis=1), ((0, 0), (0, 126)))
    attn_w = gather_wide(
        jnp.concatenate([query_weight, key_weight, value_weight, out_weight.T, gains], axis=1)
    )
    x_near, x_far = gather_halves(patches)
    mlp_w = gather_wide(jnp.concatenate([gate_weight, up_weight, down_weight.T], axis=1))
    g_near, g_far = gather_halves(cotangent)
    qkv_w = attn_w[:, : 3 * width]
    out_w = attn_w[:, 3 * width : 4 * width]
    gain_one = wide32(attn_w[:, 4 * width])[None]
    gain_two = wide32(attn_w[:, 4 * width + 1])[None]

    rows = jnp.concatenate([x_near, x_far], axis=0)
    h_one, q, k, v = project(rows, gain_one, qkv_w)
    half = rows.shape[0] // 2
    o_far, lse_far, part_far = attention_forward(scalars, q, k, v, out_w, half)
    from_far = cross(pair_sum(part_far))
    o_near, lse_near, part_near = attention_forward(scalars, q, k, v, out_w, 0)
    middle_own = wide32(patches) + pair_sum(part_near) + from_far
    m_near, m_far = gather_halves(low(middle_own))
    y_near, dh_near, h2_near, hid_near, dg_near, du_near, n2_near = mlp(m_near, g_near, gain_two, mlp_w)
    y_far, dh_far, h2_far, hid_far, dg_far, du_far, n2_far = mlp(m_far, g_far, gain_two, mlp_w)
    dh_two = pair_sum(dh_near) + cross(pair_sum(dh_far))
    middle_grad_own = wide32(cotangent) + norm_back(middle_own, gain_two, dh_two)
    d_near, d_far = gather_halves(low(middle_grad_own))
    output = low(middle_own + pair_sum(y_near) + cross(pair_sum(y_far)))
    mlp_sums = reduce_wide(
        jnp.concatenate(
            [
                dot(h2_near, dg_near, TN) + dot(h2_far, dg_far, TN),
                dot(h2_near, du_near, TN) + dot(h2_far, du_far, TN),
                dot(g_near, hid_near, TN) + dot(g_far, hid_far, TN),
            ],
            axis=1,
        )
    )
    dq_near, dk_sum, dv_sum = attention_backward(scalars, q, k, v, d_near, out_w, o_near, lse_near, ())
    dq_far, dk, dv = attention_backward(scalars, q, k, v, d_far, out_w, o_far, lse_far, (dk_sum, dv_sum))
    dh_far, n1_far = rows_back(dq_far, dk, dv, x_far, qkv_w, half)
    from_far = cross(pair_sum(dh_far))
    dh_near, n1_near = rows_back(dq_near, dk, dv, x_near, qkv_w, 0)
    dh_one = pair_sum(dh_near) + from_far
    grad_input = middle_grad_own + norm_back(wide32(patches), gain_one, dh_one)
    norms = sum_narrow(
        jnp.stack([jnp.sum(n1_near + n1_far, axis=0), jnp.sum(n2_near + n2_far, axis=0)], axis=0)
    )
    attn_sums = reduce_wide(
        jnp.concatenate(
            [
                dot(h_one, jnp.concatenate([dq_near, dq_far], axis=0), TN),
                dot(h_one, dk, TN),
                dot(h_one, dv, TN),
                dot(d_near, o_near, TN) + dot(d_far, o_far, TN),
                jnp.pad(norms.T, ((0, 0), (0, 126))),
            ],
            axis=1,
        )
    )
    return (
        output,
        grad_input,
        attn_sums[:, 4 * width],
        attn_sums[:, :width],
        attn_sums[:, width : 2 * width],
        attn_sums[:, 2 * width : 3 * width],
        attn_sums[:, 3 * width : 4 * width].T,
        attn_sums[:, 4 * width + 1],
        mlp_sums[:, :hidden_dev],
        mlp_sums[:, hidden_dev : 2 * hidden_dev],
        mlp_sums[:, 2 * hidden_dev :].T,
    )


def solution(mesh):
    tokens = P(("wide", "narrow"), None)
    return jax.shard_map(
        on_device,
        mesh=mesh,
        in_specs=(
            tokens, tokens, P("wide", None), P("wide", None), P("wide"), P("wide", "narrow"),
            P("wide", "narrow"), P("wide", "narrow"), P("narrow", "wide"), P("wide"),
            P("wide", "narrow"), P("wide", "narrow"), P("narrow", "wide"),
        ),
        out_specs=(
            tokens, tokens, P("wide"), P("wide", "narrow"), P("wide", "narrow"), P("wide", "narrow"),
            P("narrow", "wide"), P("wide"), P("wide", "narrow"), P("wide", "narrow"), P("narrow", "wide"),
        ),
        check_vma=False,
    )
```

```python
import functools

import jax
import jax.numpy as jnp
from jax import lax
from jax.experimental import pallas as pl
from jax.experimental.pallas import tpu as pltpu
from jax.sharding import PartitionSpec as P

HEAD = 64
BUCKET = 2048
EPSILON = 1e-06
MASKED = -1e30
NARROW = 4


NT = (((1,), (1,)), ((), ()))
NN = (((1,), (0,)), ((), ()))
TN = (((0,), (0,)), ((), ()))


def dot(left, right, dims=NN):
    return lax.dot_general(left, right, dims, preferred_element_type=jnp.float32)


def low(values):
    return values.astype(jnp.bfloat16)


def wide32(values):
    return values.astype(jnp.float32)


def swap(values, axis, bits):
    size = lax.axis_size(axis)
    return lax.ppermute(values, axis, [(i, i ^ bits) for i in range(size)])


def after(values, *earlier):
    return lax.optimization_barrier((values, *earlier))[0]


def gather_rows(own):
    across = swap(own, "narrow", 2)
    return own, swap(own, "narrow", 1), across, swap(across, "narrow", 1)


def pair_sum(parts):
    return wide32(parts[0]) + wide32(swap(parts[1], "narrow", 1))


def cross(values):
    return wide32(swap(low(values), "narrow", 2))


def places():
    if lax.axis_size("wide") != 8:
        return jnp.arange(8, dtype=jnp.int32)
    index = lax.axis_index("wide").astype(jnp.int32)
    order = jnp.array([0, 2, 4, 6, 1, 3, 5, 7], jnp.int32)
    return jnp.bitwise_xor(order, index)


def gather_wide(own, ready=()):
    if lax.axis_size("wide") != 8:
        return jnp.split(lax.all_gather(own, "wide", axis=0, tiled=True), 8, axis=0)
    column = [own] + [swap(own, "wide", 2 * k) for k in (1, 2, 3)]
    sent = [after(own, *ready)] + column[1:]
    return column + [swap(piece, "wide", 1) for piece in sent]


def send_x(sent):
    if lax.axis_size("wide") != 8:
        return sent
    return [swap(part, "wide", 1) for part in sent]


def add_x(kept, received):
    rows = kept[0].shape[0]
    far = [received[0][j * rows : (j + 1) * rows] for j in range(3)]
    return [low(wide32(mine) + wide32(other)) for mine, other in zip(kept, [received[1]] + far[::-1])]


def send_z(column):
    return [column[0]] + [swap(column[k], "wide", 2 * k) for k in (3, 2, 1)]


def reduce_wide(parts):
    size = lax.axis_size("wide")
    if size == 8:
        columns = [add_x(kept, received) for kept, received in parts]
        return send_z([jnp.concatenate(pieces, axis=1) for pieces in zip(*columns)])
    full = []
    for kept, sent in parts:
        rows = kept[0].shape[0]
        far = [sent[0][j * rows : (j + 1) * rows] for j in range(3)]
        full.append(jnp.concatenate(kept + [sent[1]] + far[::-1], axis=0))
    full = jnp.concatenate(full, axis=1)
    return list(lax.all_to_all(full.reshape(size, -1, full.shape[1]), "wide", 0, 0, tiled=True))


def sum_all(values):
    values = values + swap(values, "narrow", 1)
    values = values + swap(values, "narrow", 2)
    size = lax.axis_size("wide")
    if size != 8:
        values = lax.psum(values, "wide")
    else:
        for bits in (1, 2, 4):
            values = values + swap(values, "wide", bits)
    rows = values.shape[1] // size
    return lax.dynamic_slice_in_dim(values, lax.axis_index("wide") * rows, rows, 1)


def call(kernel, grid, in_specs, out_specs, out_shape, scratch=(), prefetch=0):
    return pl.pallas_call(
        kernel,
        out_shape=out_shape,
        grid_spec=pltpu.PrefetchScalarGridSpec(
            num_scalar_prefetch=prefetch,
            grid=grid,
            in_specs=in_specs,
            out_specs=out_specs,
            scratch_shapes=scratch,
        ),
        compiler_params=pltpu.CompilerParams(
            dimension_semantics=("arbitrary",) * len(grid), vmem_limit_bytes=52 << 20
        ),
    )


def by_row(block, width):
    return pl.BlockSpec((block, width), lambda i, *_: (i, 0))


def whole(*shape):
    return pl.BlockSpec(shape, lambda i, *_: (0,) * len(shape))


def shaped(shape, dtype=jnp.bfloat16):
    return jax.ShapeDtypeStruct(shape, dtype)


def inverse_rms(values):
    return lax.rsqrt(jnp.mean(values * values, axis=-1, keepdims=True) + EPSILON)


def eight(values):
    return jnp.sum(values.reshape(values.shape[0] // 8, 8, values.shape[1]), axis=0)


def parts_in(parts, block):
    per = parts[0].shape[0] // block
    width = parts[0].shape[1]

    def spec(j):
        return pl.BlockSpec((block, width), lambda i, *_: (jnp.clip(i - j * per, 0, per - 1), 0))

    return [spec(j) for j in range(len(parts))]


def pick(refs, steps):
    value = refs[0][...]
    for j in range(1, len(refs)):
        value = jnp.where(pl.program_id(0) >= j * (steps // len(refs)), refs[j][...], value)
    return value


def halves(block, width, steps):
    per = steps // 2
    return [
        pl.BlockSpec((block, width), lambda i, *_: (jnp.minimum(i, per - 1), 0)),
        pl.BlockSpec((block, width), lambda i, *_: (jnp.maximum(i - per, 0), 0)),
    ]


def put(refs, value, steps):
    @pl.when(pl.program_id(0) < steps // 2)
    def _():
        refs[0][...] = value

    @pl.when(pl.program_id(0) >= steps // 2)
    def _():
        refs[1][...] = value


def eye(size):
    return low(
        wide32(lax.broadcasted_iota(jnp.int32, (size, size), 0) == lax.broadcasted_iota(jnp.int32, (size, size), 1))
    )


def pack_kernel(q_ref, k_ref, v_ref, o_ref, g1_ref, g2_ref, gate_ref, up_ref, down_ref, a_ref, b_ref):
    rows, width = q_ref.shape
    hidden = gate_ref.shape[1]
    one = eye(rows)
    a_ref[:, :width] = q_ref[...]
    a_ref[:, width : 2 * width] = k_ref[...]
    a_ref[:, 2 * width : 3 * width] = v_ref[...]
    a_ref[:, 3 * width : 4 * width] = low(dot(one, o_ref[...], NT))
    line = lax.broadcasted_iota(jnp.int32, (a_ref.shape[1] - 4 * width, rows), 0)
    gains = jnp.where(line == 0, wide32(g1_ref[...]), jnp.where(line == 1, wide32(g2_ref[...]), 0.0))
    a_ref[:, 4 * width :] = low(dot(one, low(gains), NT))
    b_ref[:, :hidden] = gate_ref[...]
    b_ref[:, hidden : 2 * hidden] = up_ref[...]
    b_ref[:, 2 * hidden :] = down_ref[...]


def round_up(count):
    return -(-count // 128) * 128


def pack(q, k, v, o, gain_one, gain_two, gate, up, down):
    rows, width = q.shape
    first, second = round_up(4 * width + 2), 3 * gate.shape[1]
    if lax.axis_size("wide") != 8:
        a = jnp.concatenate([q, k, v, o.T, gain_one[:, None], gain_two[:, None]], axis=1)
        return jnp.pad(a, ((0, 0), (0, first - a.shape[1]))), jnp.concatenate([gate, up, down], axis=1)
    args = (q, k, v, o, gain_one[None], gain_two[None], gate, up, down)
    return call(
        pack_kernel,
        (1,),
        [whole(*arg.shape) for arg in args],
        [whole(rows, first), whole(rows, second)],
        [shaped((rows, first)), shaped((rows, second))],
    )(*args)


def lay(place_ref, pieces, target):
    rows = pieces[0].shape[0]
    for j, piece in enumerate(pieces):
        target[pl.ds(pl.multiple_of(place_ref[j] * rows, 32), rows), :] = piece[...]


def project_kernel(place_ref, *refs, width, steps):
    xs, ws, (h_ref, q_ref, k_ref, v_ref, w_ref, out_ref, gain_ref) = refs[:4], refs[4:12], refs[12:]

    @pl.when(pl.program_id(0) == 0)
    def _():
        lay(place_ref, ws, w_ref)
        out_ref[...] = w_ref[:, 3 * width : 4 * width]
        gain_ref[...] = wide32(w_ref[:, 4 * width : 4 * width + 128]).T[:8]

    x = wide32(pick(xs, steps))
    h = low(x * inverse_rms(x) * gain_ref[0:1, :])
    h_ref[...] = h
    qkv = low(dot(h, w_ref[:, : 3 * width]))
    q_ref[...] = qkv[:, :width]
    k_ref[...] = qkv[:, width : 2 * width]
    v_ref[...] = qkv[:, 2 * width :]


def project(place, rows, pieces, width, block=512):
    d, full = rows[0].shape[1], pieces[0].shape[1]
    tokens = 4 * rows[0].shape[0]
    steps = tokens // block
    return call(
        functools.partial(project_kernel, width=width, steps=steps),
        (steps,),
        parts_in(rows, block) + [whole(*piece.shape) for piece in pieces],
        [by_row(block, d)] + [by_row(block, width)] * 3 + [whole(d, full), whole(d, width), whole(8, d)],
        [shaped((tokens, d))] + [shaped((tokens, width))] * 3 + [shaped((d, full)), shaped((d, width)), shaped((8, d), jnp.float32)],
        prefetch=1,
    )(place, *rows, *pieces)


def grads_kernel(place_ref, *refs, groups, steps):
    kept, (far, fourth), total = refs[-7:-3], refs[-3:-1], refs[-1]
    refs = list(refs[:-7])
    step = pl.program_id(0)

    def take(count):
        taken = refs[:count]
        del refs[:count]
        return pick(taken, steps)

    found = []
    for lhs_parts, rhs_parts in groups:
        lhs = take(lhs_parts)
        found.append(dot(lhs, jnp.concatenate([take(count) for count in rhs_parts], axis=1), TN))

    @pl.when(step == 0)
    def _():
        total[...] = jnp.concatenate(found, axis=1)

    @pl.when(step > 0)
    def _():
        total[...] += jnp.concatenate(found, axis=1)

    @pl.when(step == steps - 1)
    def _():
        rows = fourth.shape[0]

        def piece(j):
            return low(total[pl.ds(pl.multiple_of(place_ref[j] * rows, 32), rows), :])

        for j in range(4):
            kept[j][...] = piece(j)
        for j in range(3):
            far[j * rows : (j + 1) * rows, :] = piece(7 - j)
        fourth[...] = piece(4)


def grad_pieces(place, groups, block=512):
    arrays, counts, specs, full = [], [], [], 0
    for lhs, rhs in groups:
        counts.append((len(lhs), [len(parts) for parts in rhs]))
        for parts in [lhs] + rhs:
            arrays += parts
            specs += parts_in(parts, block)
        full += sum(parts[0].shape[1] for parts in rhs)
    tokens = sum(part.shape[0] for part in groups[0][0])
    d = groups[0][0][0].shape[1]
    shapes = [(d // 8, full)] * 4 + [(3 * d // 8, full), (d // 8, full)]
    found = call(
        functools.partial(grads_kernel, groups=counts, steps=tokens // block),
        (tokens // block,),
        specs,
        [whole(*shape) for shape in shapes],
        [shaped(shape) for shape in shapes],
        scratch=[pltpu.VMEM((d, full), jnp.float32)],
        prefetch=1,
    )(place, *arrays)
    return list(found[:4]), list(found[4:])


def finish_kernel(*refs, widths):
    pieces, outs = refs[: -len(widths)], refs[-len(widths) :]
    total = wide32(pieces[0][...])
    for piece in pieces[1:]:
        total = total + wide32(piece[...])
    at = 0
    for out, width in zip(outs, widths):
        part = total[:, at : at + width]
        out[...] = part.T if out.shape[1] == part.shape[0] else part
        at += width


def finish(pieces, widths, turned):
    if len(pieces) != 4:
        cuts = [sum(widths[: j + 1]) for j in range(len(widths) - 1)]
        parts = jnp.split(sum(wide32(piece) for piece in pieces), cuts, 1)
        return (*parts[:-1], parts[-1].T) if turned else parts
    rows, full = pieces[0].shape
    shapes = [(rows, width) for width in widths[:-1]] + [(widths[-1], rows) if turned else (rows, widths[-1])]
    return call(
        functools.partial(finish_kernel, widths=widths),
        (1,),
        [whole(rows, full)] * 4,
        [whole(*shape) for shape in shapes],
        [shaped(shape, jnp.float32) for shape in shapes],
    )(*pieces)


def key_bias(len_ref, cnt_ref, own_ref, row, items):
    unit = BUCKET // NARROW
    own = own_ref[0]
    col = lax.broadcasted_iota(jnp.int32, (1, BUCKET), 1)
    col = ((col // unit) ^ own) * unit + col % unit
    row = ((row // unit) ^ own) * unit
    start = jnp.int32(0)
    low_end = jnp.int32(0)
    high_end = jnp.int32(0)
    for i in range(items):
        length = len_ref[0, i]
        inside = (row >= start) & (row < start + length)
        low_end = jnp.where(inside, start, low_end)
        high_end = jnp.where(inside, start + cnt_ref[0, i], high_end)
        start = start + length
    return jnp.where((col >= low_end) & (col < high_end), 0.0, MASKED).astype(jnp.float32)


def forward_kernel(
    len_ref, cnt_ref, own_ref, q_ref, k_ref, v_ref, o_ref, lse_ref, *, first, block, heads, items
):
    bias = key_bias(len_ref, cnt_ref, own_ref, first + pl.program_id(0) * block, items)
    for h in range(heads):
        cols = slice(h * HEAD, (h + 1) * HEAD)
        scores = dot(q_ref[:, cols], k_ref[:, cols], NT) + bias
        highest = jnp.max(scores, axis=-1, keepdims=True)
        weights = jnp.exp(scores - highest)
        total = jnp.sum(weights, axis=-1, keepdims=True)
        o_ref[:, cols] = low(dot(low(weights), v_ref[:, cols]) / total)
        lse_ref[:, h : h + 1] = highest + jnp.log(total)


def attention_forward(scalars, q, k, v, first, block=256):
    tokens, width = q.shape
    heads, items = width // HEAD, scalars[0].shape[1]
    rows = tokens // 2
    at = first // block
    row = pl.BlockSpec((block, width), lambda i, *_: (i + at, 0))
    return call(
        functools.partial(forward_kernel, first=first, block=block, heads=heads, items=items),
        (rows // block,),
        [row, whole(tokens, width), whole(tokens, width)],
        [by_row(block, width), by_row(block, heads)],
        [shaped((rows, width)), shaped((rows, heads), jnp.float32)],
        prefetch=3,
    )(*scalars, q, k, v)


def backward_kernel(
    len_ref, cnt_ref, own_ref, q_ref, k_ref, v_ref, ga_ref, gb_ref, w_ref, o_ref, lse_ref, *rest, first, block, heads, items, steps
):
    if first:
        dk_in, dv_in, dq_ref, dk_ref, dv_ref, dk_sum, dv_sum = rest
    else:
        dq_ref, dk_sum, dv_sum = rest
    step = pl.program_id(0)
    bias = key_bias(len_ref, cnt_ref, own_ref, first + step * block, items)

    @pl.when(step == 0)
    def _():
        dk_sum[...] = dk_in[...] if first else jnp.zeros_like(dk_sum)
        dv_sum[...] = dv_in[...] if first else jnp.zeros_like(dv_sum)

    do_all = low(dot(pick((ga_ref, gb_ref), steps), w_ref[:, : heads * HEAD]))
    for h in range(heads):
        cols = slice(h * HEAD, (h + 1) * HEAD)
        q, k, v, do = q_ref[:, cols], k_ref[:, cols], v_ref[:, cols], do_all[:, cols]
        delta = jnp.sum(wide32(do) * wide32(o_ref[:, cols]), axis=-1, keepdims=True)
        probs = jnp.exp(dot(q, k, NT) + bias - lse_ref[:, h : h + 1])
        ds = low(probs * (dot(do, v, NT) - delta))
        dq_ref[:, cols] = low(dot(ds, k))
        dv_sum[cols, :] += dot(do, low(probs), TN)
        dk_sum[cols, :] += dot(q, ds, TN)

    if first:

        @pl.when(step == pl.num_programs(0) - 1)
        def _():
            dk_ref[...] = low(dk_sum[...].T)
            dv_ref[...] = low(dv_sum[...].T)


def attention_backward(scalars, q, k, v, grad, out_w, o, lse, sums, block=128):
    tokens, width = q.shape
    heads, items = width // HEAD, scalars[0].shape[1]
    rows = tokens // 2
    first = rows if sums else 0
    at = first // block
    row = pl.BlockSpec((block, width), lambda i, *_: (i + at, 0))
    full = whole(tokens, width)
    turned = whole(width, tokens)
    kept = shaped((width, tokens), jnp.float32)
    in_specs = [row, full, full] + parts_in(grad, block) + [whole(*out_w.shape), by_row(block, width), by_row(block, heads)]
    return call(
        functools.partial(backward_kernel, first=first, block=block, heads=heads, items=items, steps=rows // block),
        (rows // block,),
        in_specs + ([turned, turned] if sums else []),
        [by_row(block, width)] + ([full, full] if sums else [turned, turned]),
        [shaped((rows, width))] + ([shaped((tokens, width))] * 2 if sums else [kept, kept]),
        scratch=[pltpu.VMEM((width, tokens), jnp.float32)] * 2 if sums else [],
        prefetch=3,
    )(*scalars, q, k, v, *grad, out_w, o, lse, *sums)


def mlp_kernel(place_ref, *refs, width, heads_width, steps, near):
    xs, gs, os, ws, gain_ref = refs[:2], refs[2:4], refs[4:8], refs[8:12], refs[12]
    pieces, outs = (refs[13:14], refs[14:]) if near else (refs[13:21], refs[21:])
    ys, dhs, (h_ref, hid_ref, dg_ref, du_ref, norm_ref) = outs[:2], outs[2:4], outs[4:9]
    w_ref = pieces[0] if near else outs[9]
    if not near:

        @pl.when(pl.program_id(0) == 0)
        def _():
            lay(place_ref, pieces, w_ref)

    m = wide32(pick(xs, steps))
    for o_ref, out_ref in zip(os, ws):
        m = m + dot(o_ref[...], out_ref[:, :heads_width], NT)
    if near:

        @pl.when(pl.program_id(0) < steps // 2)
        def _():
            outs[9][...] = m

    n = m * inverse_rms(m)
    h = low(n * gain_ref[1:2, :])
    h_ref[...] = h
    both = dot(h, w_ref[:, : 2 * width])
    gate, up = both[:, :width], both[:, width:]
    square = gate * gate
    scale = 0.7978845608028654
    t = jnp.tanh(scale * gate * (1.0 + 0.044715 * square))
    half = 0.5 * (1.0 + t)
    act = gate * half
    slope = half + (0.5 * scale) * gate * (1.0 - t * t) * (1.0 + 0.134145 * square)
    hid = low(act * up)
    hid_ref[...] = hid
    put(ys, low(dot(hid, w_ref[:, 2 * width :], NT)), steps)
    dhid = dot(pick(gs, steps), w_ref[:, 2 * width :])
    dgate = low(dhid * up * slope)
    dup = low(dhid * act)
    dg_ref[...] = dgate
    du_ref[...] = dup
    dh = dot(dgate, w_ref[:, :width], NT) + dot(dup, w_ref[:, width : 2 * width], NT)
    put(dhs, low(dh), steps)

    @pl.when(pl.program_id(0) == 0)
    def _():
        norm_ref[...] = jnp.zeros_like(norm_ref)

    norm_ref[...] += eight(dh * n)


def mlp(place, xs, gs, os, out_ws, gains, weight, near, block=256):
    part, d = xs[0].shape
    rows, steps = 2 * part, 2 * part // block
    width, heads_width = weight[0].shape[1] // 3, os[0].shape[1]
    wide_row, thin_row = by_row(block, d), by_row(block, width)
    split = halves(block, d, steps)
    other = pl.BlockSpec((block, heads_width), lambda i, *_: ((i + steps // 2) % steps, 0))
    out = call(
        functools.partial(mlp_kernel, width=width, heads_width=heads_width, steps=steps, near=near),
        (steps,),
        parts_in(xs, block) + parts_in(gs, block) + [by_row(block, heads_width), other] * 2
        + [whole(*out_ws[0].shape)] * 4 + [whole(8, d)] + [whole(*piece.shape) for piece in weight],
        split * 2 + [wide_row] + [thin_row] * 3 + [whole(8, d)] + (split[:1] if near else [whole(d, 3 * width)]),
        [shaped((part, d))] * 4 + [shaped((rows, d))] + [shaped((rows, width))] * 3
        + [shaped((8, d), jnp.float32)] + [shaped((part, d), jnp.float32) if near else shaped((d, 3 * width))],
        prefetch=1,
    )(place, *xs, *gs, *os, *out_ws, gains, *weight)
    return (out[:2], out[2:4]) + tuple(out[4:])


def rows_kernel(dq_ref, dk_ref, dv_ref, xa_ref, xb_ref, w_ref, dha_ref, dhb_ref, norm_ref, *, width, steps):
    dh = dot(dq_ref[...], w_ref[:, :width], NT)
    dh += dot(dk_ref[...], w_ref[:, width : 2 * width], NT)
    dh += dot(dv_ref[...], w_ref[:, 2 * width : 3 * width], NT)
    put((dha_ref, dhb_ref), low(dh), steps)
    x = wide32(pick((xa_ref, xb_ref), steps))

    @pl.when(pl.program_id(0) == 0)
    def _():
        norm_ref[...] = jnp.zeros_like(norm_ref)

    norm_ref[...] += eight(dh * x * inverse_rms(x))


def rows_back(dq, dk, dv, xs, weight, first, block=256):
    count, width = dq.shape
    part, d = xs[0].shape
    at, steps = first // block, count // block
    late = pl.BlockSpec((block, width), lambda i, *_: (i + at, 0))
    dha, dhb, norm = call(
        functools.partial(rows_kernel, width=width, steps=steps),
        (steps,),
        [by_row(block, width), late, late] + parts_in(xs, block) + [whole(*weight.shape)],
        halves(block, d, steps) + [whole(8, d)],
        [shaped((part, d))] * 2 + [shaped((8, d), jnp.float32)],
    )(dq, dk, dv, *xs, weight)
    return (dha, dhb), norm


def norm_back(values, gain, grad):
    r = inverse_rms(values)
    n = values * r
    scaled = gain * grad
    return r * (scaled - n * jnp.mean(scaled * n, axis=-1, keepdims=True))


def on_device(
    patches, cotangent, item_len, valid_count, norm1_gain, query_weight, key_weight, value_weight,
    out_weight, norm2_gain, gate_weight, up_weight, down_weight,
):
    width = query_weight.shape[1]
    hidden = gate_weight.shape[1]
    scalars = (item_len, valid_count, lax.axis_index("narrow").astype(jnp.int32).reshape(1))
    place = places()
    attn_own, mlp_own = pack(
        query_weight, key_weight, value_weight, out_weight, norm1_gain, norm2_gain,
        gate_weight, up_weight, down_weight.T,
    )
    x = gather_rows(patches)
    attn_pieces = gather_wide(attn_own)
    mlp_pieces = gather_wide(after(mlp_own, *attn_pieces[1:4]), attn_pieces[4:])
    g = gather_rows(after(cotangent, *attn_pieces[1:4]))

    h_one, q, k, v, qkv_w, out_w, gains = project(place, x, attn_pieces, width)
    out_ws = gather_rows(after(out_w, g[2]))
    half = q.shape[0] // 2
    o_near, lse_near = attention_forward(scalars, q, k, v, 0)
    o_far_across = swap(o_near, "narrow", 2)
    o_far_across = (o_far_across, swap(o_far_across, "narrow", 1))
    o_far, lse_far = attention_forward(scalars, q, k, v, half)
    o_near_across = swap(o_far, "narrow", 2)
    o_far_all = (o_far, swap(o_far, "narrow", 1)) + o_far_across
    o_near_all = (o_near, swap(o_near, "narrow", 1), o_near_across, swap(o_near_across, "narrow", 1))
    y_far, dh_far, h2_far, hid_far, dg_far, du_far, n2_far, mlp_w = mlp(
        place, x[2:], g[2:], o_far_all, out_ws, gains, mlp_pieces, False
    )
    from_far = cross(pair_sum(dh_far))
    y_near, dh_near, h2_near, hid_near, dg_near, du_near, n2_near, middle_own = mlp(
        place, x[:2], g[:2], o_near_all, out_ws, gains, [mlp_w], True
    )
    gain_one, gain_two = gains[0:1], gains[1:2]
    dh_two = pair_sum(dh_near) + from_far
    mlp_parts = grad_pieces(
        place,
        [([h2_near, h2_far], [[dg_near, dg_far], [du_near, du_far]]), (list(g), [[hid_near, hid_far]])],
    )
    mlp_sent = send_x(mlp_parts[1])
    middle_grad_own = wide32(cotangent) + norm_back(middle_own, gain_two, dh_two)
    d = gather_rows(low(middle_grad_own))
    grad_gate, grad_up, grad_down = finish(reduce_wide([(mlp_parts[0], mlp_sent)]), (hidden, hidden, hidden), False)
    dq_near, dk_sum, dv_sum = attention_backward(scalars, q, k, v, d[:2], out_w, o_near, lse_near, ())
    output = low(middle_own + pair_sum(y_near) + cross(after(pair_sum(y_far), d[2])))
    out_parts = grad_pieces(place, [(list(d), [[o_near, o_far]])])
    out_sent = send_x(out_parts[1])
    dq_far, dk, dv = attention_backward(scalars, q, k, v, d[2:], out_w, o_far, lse_far, (dk_sum, dv_sum))
    attn_parts = grad_pieces(place, [([h_one], [[dq_near, dq_far], [dk], [dv]])])
    attn_sent = send_x(attn_parts[1])
    dh_far, n1_far = rows_back(dq_far, dk, dv, x[2:], qkv_w, half)
    from_far = cross(pair_sum(dh_far))
    dh_near, n1_near = rows_back(dq_near, dk, dv, x[:2], qkv_w, 0)
    grad_query, grad_key, grad_value, grad_out = finish(
        reduce_wide([(attn_parts[0], attn_sent), (out_parts[0], out_sent)]), (width, width, width, width), True
    )
    dh_one = pair_sum(dh_near) + from_far
    grad_input = middle_grad_own + norm_back(wide32(patches), gain_one, dh_one)
    norms = sum_all(
        jnp.stack([jnp.sum(n1_near + n1_far, axis=0), jnp.sum(n2_near + n2_far, axis=0)], axis=0)
    )
    return (
        output, grad_input, norms[0], grad_query, grad_key, grad_value, grad_out, norms[1],
        grad_gate, grad_up, grad_down.T,
    )


def solution(mesh):
    tokens = P(("wide", "narrow"), None)

    return jax.shard_map(
        on_device,
        mesh=mesh,
        in_specs=(
            tokens, tokens, P("wide", None), P("wide", None), P("wide"), P("wide", "narrow"),
            P("wide", "narrow"), P("wide", "narrow"), P("narrow", "wide"), P("wide"),
            P("wide", "narrow"), P("wide", "narrow"), P("narrow", "wide"),
        ),
        out_specs=(
            tokens, tokens, P("wide"), P("wide", "narrow"), P("wide", "narrow"), P("wide", "narrow"),
            P("narrow", "wide"), P("wide"), P("wide", "narrow"), P("wide", "narrow"), P("narrow", "wide"),
        ),
        check_vma=False,
    )
```

```python
import functools

import jax
import jax.numpy as jnp
from jax import lax
from jax.experimental import pallas as pl
from jax.experimental.pallas import tpu as pltpu
from jax.sharding import PartitionSpec as P

HEAD = 64
BUCKET = 2048
EPSILON = 1e-06
MASKED = -1e30
NARROW = 4


NT = (((1,), (1,)), ((), ()))
NN = (((1,), (0,)), ((), ()))
TN = (((0,), (0,)), ((), ()))


def dot(left, right, dims=NN):
    return lax.dot_general(left, right, dims, preferred_element_type=jnp.float32)


def low(values):
    return values.astype(jnp.bfloat16)


def wide32(values):
    return values.astype(jnp.float32)


def swap(values, axis, bits):
    size = lax.axis_size(axis)
    return lax.ppermute(values, axis, [(i, i ^ bits) for i in range(size)])


def after(values, *earlier):
    return lax.optimization_barrier((values, *earlier))[0]


def gather_rows(own, ready=()):
    across = swap(own, "narrow", 2)
    near, far = after(own, *ready), after(across, *ready)
    return own, swap(near, "narrow", 1), across, swap(far, "narrow", 1)


def pair_sum(parts):
    return wide32(parts[0]) + wide32(swap(parts[1], "narrow", 1))


def cross(values):
    return wide32(swap(low(values), "narrow", 2))


def places():
    if lax.axis_size("wide") != 8:
        return jnp.arange(8, dtype=jnp.int32)
    index = lax.axis_index("wide").astype(jnp.int32)
    order = jnp.array([0, 2, 4, 6, 1, 3, 5, 7], jnp.int32)
    return jnp.bitwise_xor(order, index)


def gather_wide(own, ready=()):
    if lax.axis_size("wide") != 8:
        return jnp.split(lax.all_gather(own, "wide", axis=0, tiled=True), 8, axis=0)
    column = [own] + [swap(own, "wide", 2 * k) for k in (1, 2, 3)]
    sent = [after(own, *ready)] + column[1:]
    return column + [swap(piece, "wide", 1) for piece in sent]


def send_x(sent):
    if lax.axis_size("wide") != 8:
        return sent
    return [swap(part, "wide", 1) for part in sent]


def add_x(kept, received):
    rows = kept[0].shape[0]
    far = [received[0][j * rows : (j + 1) * rows] for j in range(3)]
    return [low(wide32(mine) + wide32(other)) for mine, other in zip(kept, [received[1]] + far[::-1])]


def send_z(column):
    return [column[0]] + [swap(column[k], "wide", 2 * k) for k in (3, 2, 1)]


def reduce_wide(parts):
    size = lax.axis_size("wide")
    if size == 8:
        columns = [add_x(kept, received) for kept, received in parts]
        return send_z([jnp.concatenate(pieces, axis=1) for pieces in zip(*columns)])
    full = []
    for kept, sent in parts:
        rows = kept[0].shape[0]
        far = [sent[0][j * rows : (j + 1) * rows] for j in range(3)]
        full.append(jnp.concatenate(kept + [sent[1]] + far[::-1], axis=0))
    full = jnp.concatenate(full, axis=1)
    return list(lax.all_to_all(full.reshape(size, -1, full.shape[1]), "wide", 0, 0, tiled=True))


def sum_all(values):
    values = values + swap(values, "narrow", 2)
    values = values + swap(values, "narrow", 1)
    size = lax.axis_size("wide")
    if size != 8:
        values = lax.psum(values, "wide")
    else:
        for bits in (2, 4, 1):
            values = values + swap(values, "wide", bits)
    rows = values.shape[1] // size
    return lax.dynamic_slice_in_dim(values, lax.axis_index("wide") * rows, rows, 1)


def call(kernel, grid, in_specs, out_specs, out_shape, scratch=(), prefetch=0):
    return pl.pallas_call(
        kernel,
        out_shape=out_shape,
        grid_spec=pltpu.PrefetchScalarGridSpec(
            num_scalar_prefetch=prefetch,
            grid=grid,
            in_specs=in_specs,
            out_specs=out_specs,
            scratch_shapes=scratch,
        ),
        compiler_params=pltpu.CompilerParams(
            dimension_semantics=("arbitrary",) * len(grid), vmem_limit_bytes=52 << 20
        ),
    )


def by_row(block, width):
    return pl.BlockSpec((block, width), lambda i, *_: (i, 0))


def whole(*shape):
    return pl.BlockSpec(shape, lambda i, *_: (0,) * len(shape))


def shaped(shape, dtype=jnp.bfloat16):
    return jax.ShapeDtypeStruct(shape, dtype)


def inverse_rms(values):
    return lax.rsqrt(jnp.mean(values * values, axis=-1, keepdims=True) + EPSILON)


def parts_in(parts, block):
    per = parts[0].shape[0] // block
    width = parts[0].shape[1]

    def spec(j):
        return pl.BlockSpec((block, width), lambda i, *_: (jnp.clip(i - j * per, 0, per - 1), 0))

    return [spec(j) for j in range(len(parts))]


def pick(refs, steps):
    value = refs[0][...]
    for j in range(1, len(refs)):
        value = jnp.where(pl.program_id(0) >= j * (steps // len(refs)), refs[j][...], value)
    return value


def halves(block, width, steps):
    per = steps // 2
    return [
        pl.BlockSpec((block, width), lambda i, *_: (jnp.minimum(i, per - 1), 0)),
        pl.BlockSpec((block, width), lambda i, *_: (jnp.maximum(i - per, 0), 0)),
    ]


def put(refs, value, steps):
    @pl.when(pl.program_id(0) < steps // 2)
    def _():
        refs[0][...] = value

    @pl.when(pl.program_id(0) >= steps // 2)
    def _():
        refs[1][...] = value


def eye(size):
    return low(
        wide32(lax.broadcasted_iota(jnp.int32, (size, size), 0) == lax.broadcasted_iota(jnp.int32, (size, size), 1))
    )


def pack_kernel(*refs):
    sources, (a_ref, b_ref), held, done = refs[:9], refs[9:11], refs[11:20], refs[20]
    copies = [pltpu.make_async_copy(src, dst, done.at[j]) for j, (src, dst) in enumerate(zip(sources, held))]
    for copy in copies:
        copy.start()
    for copy in copies:
        copy.wait()
    q_ref, k_ref, v_ref, o_ref, g1_ref, g2_ref, gate_ref, up_ref, down_ref = held
    rows, width = q_ref.shape
    hidden = gate_ref.shape[1]
    one = eye(rows)
    a_ref[:, :width] = q_ref[...]
    a_ref[:, width : 2 * width] = k_ref[...]
    a_ref[:, 2 * width : 3 * width] = v_ref[...]
    a_ref[:, 3 * width : 4 * width] = low(dot(one, o_ref[...], NT))
    line = lax.broadcasted_iota(jnp.int32, (a_ref.shape[1] - 4 * width, rows), 0)
    gains = jnp.where(line == 0, wide32(g1_ref[...]), jnp.where(line == 1, wide32(g2_ref[...]), 0.0))
    a_ref[:, 4 * width :] = low(dot(one, low(gains), NT))
    b_ref[:, :hidden] = gate_ref[...]
    b_ref[:, hidden : 2 * hidden] = up_ref[...]
    b_ref[:, 2 * hidden :] = down_ref[...]


def round_up(count):
    return -(-count // 128) * 128


def pack(q, k, v, o, gain_one, gain_two, gate, up, down):
    rows, width = q.shape
    first, second = round_up(4 * width + 2), 3 * gate.shape[1]
    if lax.axis_size("wide") != 8:
        a = jnp.concatenate([q, k, v, o.T, gain_one[:, None], gain_two[:, None]], axis=1)
        return jnp.pad(a, ((0, 0), (0, first - a.shape[1]))), jnp.concatenate([gate, up, down], axis=1)
    args = (q, k, v, o, gain_one[None], gain_two[None], gate, up, down)
    return call(
        pack_kernel,
        (1,),
        [pl.BlockSpec(memory_space=pltpu.HBM)] * len(args),
        [whole(rows, first), whole(rows, second)],
        [shaped((rows, first)), shaped((rows, second))],
        scratch=[pltpu.VMEM(arg.shape, arg.dtype) for arg in args] + [pltpu.SemaphoreType.DMA((len(args),))],
    )(*args)


def lay(place_ref, pieces, target):
    rows = pieces[0].shape[0]
    for j, piece in enumerate(pieces):
        target[pl.ds(pl.multiple_of(place_ref[j] * rows, 32), rows), :] = piece[...]


def project_kernel(place_ref, *refs, width, steps):
    xs, ws, (h_ref, q_ref, k_ref, v_ref, w_ref, out_ref, gain_ref) = refs[:4], refs[4:12], refs[12:]

    @pl.when(pl.program_id(0) == 0)
    def _():
        lay(place_ref, ws, w_ref)
        out_ref[...] = w_ref[:, 3 * width : 4 * width]
        gain_ref[...] = wide32(w_ref[:, 4 * width : 4 * width + 128]).T[:8]

    x = wide32(pick(xs, steps))
    h = low(x * inverse_rms(x) * gain_ref[0:1, :])
    h_ref[...] = h
    qkv = low(dot(h, w_ref[:, : 3 * width]))
    q_ref[...] = qkv[:, :width]
    k_ref[...] = qkv[:, width : 2 * width]
    v_ref[...] = qkv[:, 2 * width :]


def project(place, rows, pieces, width, block=512):
    d, full = rows[0].shape[1], pieces[0].shape[1]
    tokens = 4 * rows[0].shape[0]
    steps = tokens // block
    return call(
        functools.partial(project_kernel, width=width, steps=steps),
        (steps,),
        parts_in(rows, block) + [whole(*piece.shape) for piece in pieces],
        [by_row(block, d)] + [by_row(block, width)] * 3 + [whole(d, full), whole(d, width), whole(8, d)],
        [shaped((tokens, d))] + [shaped((tokens, width))] * 3 + [shaped((d, full)), shaped((d, width)), shaped((8, d), jnp.float32)],
        prefetch=1,
    )(place, *rows, *pieces)


def grads_kernel(place_ref, *refs, groups, steps, gain):
    if gain is not None:
        w_ref, gain_ref, norm_ref = refs[0], refs[1], refs[-2]
        refs = refs[2:-2] + refs[-1:]
    kept, (far, fourth), total = refs[-7:-3], refs[-3:-1], refs[-1]
    refs = list(refs[:-7])
    step = pl.program_id(0)

    def take(count):
        taken = refs[:count]
        del refs[:count]
        return pick(taken, steps)

    found = []
    for lhs_parts, rhs_parts in groups:
        lhs = take(lhs_parts)
        found.append(dot(lhs, jnp.concatenate([take(count) for count in rhs_parts], axis=1), TN))

    @pl.when(step == 0)
    def _():
        total[...] = jnp.concatenate(found, axis=1)

    @pl.when(step > 0)
    def _():
        total[...] += jnp.concatenate(found, axis=1)

    @pl.when(step == steps - 1)
    def _():
        rows = fourth.shape[0]

        def piece(j):
            return low(total[pl.ds(pl.multiple_of(place_ref[j] * rows, 32), rows), :])

        for j in range(4):
            kept[j][...] = piece(j)
        for j in range(3):
            far[j * rows : (j + 1) * rows, :] = piece(7 - j)
        fourth[...] = piece(4)
        if gain is not None:
            row, width = gain
            column = jnp.sum(wide32(w_ref[:, :width]) * total[:, :width], axis=1, keepdims=True)
            turned = jnp.broadcast_to(column, (column.shape[0], 128)).T
            norm_ref[...] = turned[:8] / gain_ref[row : row + 1, :]


def grad_pieces(place, groups, norm=None, block=512):
    arrays, counts, specs, full = [], [], [], 0
    if norm:
        arrays += norm[:2]
        specs += [whole(*array.shape) for array in norm[:2]]
    for lhs, rhs in groups:
        counts.append((len(lhs), [len(parts) for parts in rhs]))
        for parts in [lhs] + rhs:
            arrays += parts
            specs += parts_in(parts, block)
        full += sum(parts[0].shape[1] for parts in rhs)
    tokens = sum(part.shape[0] for part in groups[0][0])
    d = groups[0][0][0].shape[1]
    shapes = [(d // 8, full)] * 4 + [(3 * d // 8, full), (d // 8, full)]
    found = call(
        functools.partial(grads_kernel, groups=counts, steps=tokens // block, gain=norm[2:] if norm else None),
        (tokens // block,),
        specs,
        [whole(*shape) for shape in shapes] + [whole(8, d)] * bool(norm),
        [shaped(shape) for shape in shapes] + [shaped((8, d), jnp.float32)] * bool(norm),
        scratch=[pltpu.VMEM((d, full), jnp.float32)],
        prefetch=1,
    )(place, *arrays)
    return list(found[:4]), list(found[4:6]), *found[6:]


def finish_kernel(*refs, widths):
    pieces, outs = refs[: -len(widths)], refs[-len(widths) :]
    total = wide32(pieces[0][...])
    for piece in pieces[1:]:
        total = total + wide32(piece[...])
    at = 0
    for out, width in zip(outs, widths):
        part = total[:, at : at + width]
        out[...] = part.T if out.shape[1] == part.shape[0] else part
        at += width


def finish(pieces, widths, turned):
    if len(pieces) != 4:
        cuts = [sum(widths[: j + 1]) for j in range(len(widths) - 1)]
        parts = jnp.split(sum(wide32(piece) for piece in pieces), cuts, 1)
        return (*parts[:-1], parts[-1].T) if turned else parts
    rows, full = pieces[0].shape
    shapes = [(rows, width) for width in widths[:-1]] + [(widths[-1], rows) if turned else (rows, widths[-1])]
    return call(
        functools.partial(finish_kernel, widths=widths),
        (1,),
        [whole(rows, full)] * 4,
        [whole(*shape) for shape in shapes],
        [shaped(shape, jnp.float32) for shape in shapes],
    )(*pieces)


def key_bias(len_ref, cnt_ref, own_ref, row, items):
    unit = BUCKET // NARROW
    own = own_ref[0]
    col = lax.broadcasted_iota(jnp.int32, (1, BUCKET), 1)
    col = ((col // unit) ^ own) * unit + col % unit
    row = ((row // unit) ^ own) * unit
    start = jnp.int32(0)
    low_end = jnp.int32(0)
    high_end = jnp.int32(0)
    for i in range(items):
        length = len_ref[0, i]
        inside = (row >= start) & (row < start + length)
        low_end = jnp.where(inside, start, low_end)
        high_end = jnp.where(inside, start + cnt_ref[0, i], high_end)
        start = start + length
    return jnp.where((col >= low_end) & (col < high_end), 0.0, MASKED).astype(jnp.float32)


def forward_kernel(
    len_ref, cnt_ref, own_ref, q_ref, k_ref, v_ref, o_ref, lse_ref, *, first, block, heads, items
):
    bias = key_bias(len_ref, cnt_ref, own_ref, first + pl.program_id(0) * block, items)
    for h in range(heads):
        cols = slice(h * HEAD, (h + 1) * HEAD)
        scores = dot(q_ref[:, cols], k_ref[:, cols], NT) + bias
        highest = jnp.max(scores, axis=-1, keepdims=True)
        weights = jnp.exp(scores - highest)
        total = jnp.sum(weights, axis=-1, keepdims=True)
        o_ref[:, cols] = low(dot(low(weights), v_ref[:, cols]) / total)
        lse_ref[:, h : h + 1] = highest + jnp.log(total)


def attention_forward(scalars, q, k, v, first, block=256):
    tokens, width = q.shape
    heads, items = width // HEAD, scalars[0].shape[1]
    rows = tokens // 2
    at = first // block
    row = pl.BlockSpec((block, width), lambda i, *_: (i + at, 0))
    return call(
        functools.partial(forward_kernel, first=first, block=block, heads=heads, items=items),
        (rows // block,),
        [row, whole(tokens, width), whole(tokens, width)],
        [by_row(block, width), by_row(block, heads)],
        [shaped((rows, width)), shaped((rows, heads), jnp.float32)],
        prefetch=3,
    )(*scalars, q, k, v)


def backward_kernel(
    len_ref, cnt_ref, own_ref, q_ref, k_ref, v_ref, ga_ref, gb_ref, w_ref, o_ref, lse_ref, *rest, first, block, heads, items, steps
):
    if first:
        dk_in, dv_in, dq_ref, dk_ref, dv_ref, dk_sum, dv_sum = rest
    else:
        dq_ref, dk_sum, dv_sum = rest
    step = pl.program_id(0)
    bias = key_bias(len_ref, cnt_ref, own_ref, first + step * block, items)

    @pl.when(step == 0)
    def _():
        dk_sum[...] = dk_in[...] if first else jnp.zeros_like(dk_sum)
        dv_sum[...] = dv_in[...] if first else jnp.zeros_like(dv_sum)

    do_all = low(dot(pick((ga_ref, gb_ref), steps), w_ref[:, : heads * HEAD]))
    for h in range(heads):
        cols = slice(h * HEAD, (h + 1) * HEAD)
        q, k, v, do = q_ref[:, cols], k_ref[:, cols], v_ref[:, cols], do_all[:, cols]
        delta = jnp.sum(wide32(do) * wide32(o_ref[:, cols]), axis=-1, keepdims=True)
        probs = jnp.exp(dot(q, k, NT) + bias - lse_ref[:, h : h + 1])
        ds = low(probs * (dot(do, v, NT) - delta))
        dq_ref[:, cols] = low(dot(ds, k))
        dv_sum[cols, :] += dot(do, low(probs), TN)
        dk_sum[cols, :] += dot(q, ds, TN)

    if first:

        @pl.when(step == pl.num_programs(0) - 1)
        def _():
            dk_ref[...] = low(dk_sum[...].T)
            dv_ref[...] = low(dv_sum[...].T)


def attention_backward(scalars, q, k, v, grad, out_w, o, lse, sums, block=128):
    tokens, width = q.shape
    heads, items = width // HEAD, scalars[0].shape[1]
    rows = tokens // 2
    first = rows if sums else 0
    at = first // block
    row = pl.BlockSpec((block, width), lambda i, *_: (i + at, 0))
    full = whole(tokens, width)
    turned = whole(width, tokens)
    kept = shaped((width, tokens), jnp.float32)
    in_specs = [row, full, full] + parts_in(grad, block) + [whole(*out_w.shape), by_row(block, width), by_row(block, heads)]
    return call(
        functools.partial(backward_kernel, first=first, block=block, heads=heads, items=items, steps=rows // block),
        (rows // block,),
        in_specs + ([turned, turned] if sums else []),
        [by_row(block, width)] + ([full, full] if sums else [turned, turned]),
        [shaped((rows, width))] + ([shaped((tokens, width))] * 2 if sums else [kept, kept]),
        scratch=[pltpu.VMEM((width, tokens), jnp.float32)] * 2 if sums else [],
        prefetch=3,
    )(*scalars, q, k, v, *grad, out_w, o, lse, *sums)


def mlp_kernel(place_ref, *refs, width, heads_width, steps, near):
    xs, gs, os, ws, gain_ref = refs[:2], refs[2:4], refs[4:8], refs[8:12], refs[12]
    pieces, outs = (refs[13:14], refs[14:]) if near else (refs[13:21], refs[21:])
    ys, dhs, (h_ref, hid_ref, dg_ref, du_ref) = outs[:2], outs[2:4], outs[4:8]
    w_ref = pieces[0] if near else outs[8]
    if not near:

        @pl.when(pl.program_id(0) == 0)
        def _():
            lay(place_ref, pieces, w_ref)

    m = wide32(pick(xs, steps))
    for o_ref, out_ref in zip(os, ws):
        m = m + dot(o_ref[...], out_ref[:, :heads_width], NT)
    if near:

        @pl.when(pl.program_id(0) < steps // 2)
        def _():
            outs[8][...] = m

    n = m * inverse_rms(m)
    h = low(n * gain_ref[1:2, :])
    h_ref[...] = h
    both = dot(h, w_ref[:, : 2 * width])
    gate, up = both[:, :width], both[:, width:]
    square = gate * gate
    scale = 0.7978845608028654
    t = jnp.tanh(scale * gate * (1.0 + 0.044715 * square))
    half = 0.5 * (1.0 + t)
    act = gate * half
    slope = half + (0.5 * scale) * gate * (1.0 - t * t) * (1.0 + 0.134145 * square)
    hid = low(act * up)
    hid_ref[...] = hid
    put(ys, low(dot(hid, w_ref[:, 2 * width :], NT)), steps)
    dhid = dot(pick(gs, steps), w_ref[:, 2 * width :])
    dgate = low(dhid * up * slope)
    dup = low(dhid * act)
    dg_ref[...] = dgate
    du_ref[...] = dup
    dh = dot(dgate, w_ref[:, :width], NT) + dot(dup, w_ref[:, width : 2 * width], NT)
    put(dhs, low(dh), steps)


def mlp(place, xs, gs, os, out_ws, gains, weight, near, block=256):
    part, d = xs[0].shape
    rows, steps = 2 * part, 2 * part // block
    width, heads_width = weight[0].shape[1] // 3, os[0].shape[1]
    wide_row, thin_row = by_row(block, d), by_row(block, width)
    split = halves(block, d, steps)
    other = pl.BlockSpec((block, heads_width), lambda i, *_: ((i + steps // 2) % steps, 0))
    out = call(
        functools.partial(mlp_kernel, width=width, heads_width=heads_width, steps=steps, near=near),
        (steps,),
        parts_in(xs, block) + parts_in(gs, block) + [by_row(block, heads_width), other] * 2
        + [whole(*out_ws[0].shape)] * 4 + [whole(8, d)] + [whole(*piece.shape) for piece in weight],
        split * 2 + [wide_row] + [thin_row] * 3 + (split[:1] if near else [whole(d, 3 * width)]),
        [shaped((part, d))] * 4 + [shaped((rows, d))] + [shaped((rows, width))] * 3
        + [shaped((part, d), jnp.float32) if near else shaped((d, 3 * width))],
        prefetch=1,
    )(place, *xs, *gs, *os, *out_ws, gains, *weight)
    return (out[:2], out[2:4]) + tuple(out[4:])


def rows_kernel(dq_ref, dk_ref, dv_ref, w_ref, dha_ref, dhb_ref, *, width, steps):
    dh = dot(dq_ref[...], w_ref[:, :width], NT)
    dh += dot(dk_ref[...], w_ref[:, width : 2 * width], NT)
    dh += dot(dv_ref[...], w_ref[:, 2 * width : 3 * width], NT)
    put((dha_ref, dhb_ref), low(dh), steps)


def rows_back(dq, dk, dv, weight, first, block=512):
    count, width = dq.shape
    d = weight.shape[0]
    at, steps = first // block, count // block
    late = pl.BlockSpec((block, width), lambda i, *_: (i + at, 0))
    return call(
        functools.partial(rows_kernel, width=width, steps=steps),
        (steps,),
        [by_row(block, width), late, late, whole(*weight.shape)],
        halves(block, d, steps),
        [shaped((count // 2, d))] * 2,
    )(dq, dk, dv, weight)


def norm_back(values, gain, grad):
    r = inverse_rms(values)
    n = values * r
    scaled = gain * grad
    return r * (scaled - n * jnp.mean(scaled * n, axis=-1, keepdims=True))


def on_device(
    patches, cotangent, item_len, valid_count, norm1_gain, query_weight, key_weight, value_weight,
    out_weight, norm2_gain, gate_weight, up_weight, down_weight,
):
    width = query_weight.shape[1]
    hidden = gate_weight.shape[1]
    scalars = (item_len, valid_count, lax.axis_index("narrow").astype(jnp.int32).reshape(1))
    place = places()
    attn_own, mlp_own = pack(
        query_weight, key_weight, value_weight, out_weight, norm1_gain, norm2_gain,
        gate_weight, up_weight, down_weight.T,
    )
    attn_pieces = gather_wide(attn_own)
    x = gather_rows(patches, attn_pieces[2:3])
    mlp_pieces = gather_wide(after(mlp_own, *attn_pieces[1:4]), attn_pieces[4:])
    g = gather_rows(after(cotangent, *attn_pieces[1:4]))

    h_one, q, k, v, qkv_w, out_w, gains = project(place, x, attn_pieces, width)
    out_ws = gather_rows(after(out_w, g[2]))
    half = q.shape[0] // 2
    o_near, lse_near = attention_forward(scalars, q, k, v, 0)
    o_far_across = swap(o_near, "narrow", 2)
    o_far_across = (o_far_across, swap(o_far_across, "narrow", 1))
    o_far, lse_far = attention_forward(scalars, q, k, v, half)
    o_near_across = swap(o_far, "narrow", 2)
    o_far_all = (o_far, swap(o_far, "narrow", 1)) + o_far_across
    o_near_all = (o_near, swap(o_near, "narrow", 1), o_near_across, swap(o_near_across, "narrow", 1))
    y_far, dh_far, h2_far, hid_far, dg_far, du_far, mlp_w = mlp(
        place, x[2:], g[2:], o_far_all, out_ws, gains, mlp_pieces, False
    )
    from_far = cross(pair_sum(dh_far))
    y_near, dh_near, h2_near, hid_near, dg_near, du_near, middle_own = mlp(
        place, x[:2], g[:2], o_near_all, out_ws, gains, [mlp_w], True
    )
    gain_one, gain_two = gains[0:1], gains[1:2]
    dh_two = pair_sum(dh_near) + from_far
    mlp_kept, mlp_sent, norm_two = grad_pieces(
        place,
        [([h2_near, h2_far], [[dg_near, dg_far], [du_near, du_far]]), (list(g), [[hid_near, hid_far]])],
        [mlp_w, gains, 1, 2 * hidden],
    )
    mlp_sent = send_x(mlp_sent)
    middle_grad_own = wide32(cotangent) + norm_back(middle_own, gain_two, dh_two)
    d = gather_rows(low(middle_grad_own))
    mlp_pieces = reduce_wide([(mlp_kept, mlp_sent)])
    grad_gate, grad_up, grad_down = finish(mlp_pieces, (hidden, hidden, hidden), False)
    dq_near, dk_sum, dv_sum = attention_backward(scalars, q, k, v, d[:2], out_w, o_near, lse_near, ())
    output = low(middle_own + pair_sum(y_near) + cross(after(pair_sum(y_far), d[2])))
    out_kept, out_sent = grad_pieces(place, [(list(d), [[o_near, o_far]])])
    out_sent = send_x(out_sent)
    dq_far, dk, dv = attention_backward(scalars, q, k, v, d[2:], out_w, o_far, lse_far, (dk_sum, dv_sum))
    attn_kept, attn_sent, norm_one = grad_pieces(
        place, [([h_one], [[dq_near, dq_far], [dk], [dv]])], [qkv_w, gains, 0, 3 * width]
    )
    attn_sent = send_x(attn_sent)
    norms = sum_all(jnp.concatenate([norm_one[:1], norm_two[:1]], axis=0))
    dh_far = rows_back(dq_far, dk, dv, qkv_w, half)
    from_far = cross(pair_sum(dh_far))
    dh_near = rows_back(dq_near, dk, dv, qkv_w, 0)
    grad_query, grad_key, grad_value, grad_out = finish(
        reduce_wide([(attn_kept, attn_sent), (out_kept, out_sent)]), (width, width, width, width), True
    )
    dh_one = pair_sum(dh_near) + from_far
    grad_input = middle_grad_own + norm_back(wide32(patches), gain_one, dh_one)
    return (
        output, grad_input, norms[0], grad_query, grad_key, grad_value, grad_out, norms[1],
        grad_gate, grad_up, grad_down.T,
    )


def solution(mesh):
    tokens = P(("wide", "narrow"), None)

    return jax.shard_map(
        on_device,
        mesh=mesh,
        in_specs=(
            tokens, tokens, P("wide", None), P("wide", None), P("wide"), P("wide", "narrow"),
            P("wide", "narrow"), P("wide", "narrow"), P("narrow", "wide"), P("wide"),
            P("wide", "narrow"), P("wide", "narrow"), P("narrow", "wide"),
        ),
        out_specs=(
            tokens, tokens, P("wide"), P("wide", "narrow"), P("wide", "narrow"), P("wide", "narrow"),
            P("narrow", "wide"), P("wide"), P("wide", "narrow"), P("wide", "narrow"), P("narrow", "wide"),
        ),
        check_vma=False,
    )
```

```python
import functools

import jax
import jax.numpy as jnp
from jax import lax
from jax.experimental import pallas as pl
from jax.experimental.pallas import tpu as pltpu
from jax.sharding import PartitionSpec as P

HEAD = 64
BUCKET = 2048
EPSILON = 1e-06
MASKED = -1e30
NARROW = 4


NT = (((1,), (1,)), ((), ()))
NN = (((1,), (0,)), ((), ()))
TN = (((0,), (0,)), ((), ()))


def dot(left, right, dims=NN):
    return lax.dot_general(left, right, dims, preferred_element_type=jnp.float32)


def low(values):
    return values.astype(jnp.bfloat16)


def wide32(values):
    return values.astype(jnp.float32)


def swap(values, axis, bits):
    size = lax.axis_size(axis)
    return lax.ppermute(values, axis, [(i, i ^ bits) for i in range(size)])


def after(values, *earlier):
    return lax.optimization_barrier((values, *earlier))[0]


def gather_rows(own, ready=()):
    across = swap(own, "narrow", 2)
    near, far = after(own, *ready), after(across, *ready)
    return own, swap(near, "narrow", 1), across, swap(far, "narrow", 1)


def pair_sum(parts):
    return wide32(parts[0]) + wide32(swap(parts[1], "narrow", 1))


def cross(values):
    return wide32(swap(low(values), "narrow", 2))


def places():
    if lax.axis_size("wide") != 8:
        return jnp.arange(8, dtype=jnp.int32)
    index = lax.axis_index("wide").astype(jnp.int32)
    order = jnp.array([0, 2, 4, 6, 1, 3, 5, 7], jnp.int32)
    return jnp.bitwise_xor(order, index)


def gather_wide(own, ready=()):
    if lax.axis_size("wide") != 8:
        return jnp.split(lax.all_gather(own, "wide", axis=0, tiled=True), 8, axis=0)
    column = [own] + [swap(own, "wide", 2 * k) for k in (1, 2, 3)]
    sent = [after(own, *ready)] + column[1:]
    return column + [swap(piece, "wide", 1) for piece in sent]


def send_x(sent):
    if lax.axis_size("wide") != 8:
        return sent
    return [swap(part, "wide", 1) for part in sent]


def add_x(kept, received):
    rows = kept[0].shape[0]
    far = [received[0][j * rows : (j + 1) * rows] for j in range(3)]
    return [low(wide32(mine) + wide32(other)) for mine, other in zip(kept, [received[1]] + far[::-1])]


def send_z(column):
    return [column[0]] + [swap(column[k], "wide", 2 * k) for k in (3, 2, 1)]


def reduce_wide(parts):
    size = lax.axis_size("wide")
    if size == 8:
        columns = [add_x(kept, received) for kept, received in parts]
        return send_z([jnp.concatenate(pieces, axis=1) for pieces in zip(*columns)])
    full = []
    for kept, sent in parts:
        rows = kept[0].shape[0]
        far = [sent[0][j * rows : (j + 1) * rows] for j in range(3)]
        full.append(jnp.concatenate(kept + [sent[1]] + far[::-1], axis=0))
    full = jnp.concatenate(full, axis=1)
    return list(lax.all_to_all(full.reshape(size, -1, full.shape[1]), "wide", 0, 0, tiled=True))


def sum_all(values):
    values = values + swap(values, "narrow", 2)
    values = values + swap(values, "narrow", 1)
    size = lax.axis_size("wide")
    if size != 8:
        values = lax.psum(values, "wide")
    else:
        for bits in (2, 4, 1):
            values = values + swap(values, "wide", bits)
    rows = values.shape[1] // size
    return lax.dynamic_slice_in_dim(values, lax.axis_index("wide") * rows, rows, 1)


def call(kernel, grid, in_specs, out_specs, out_shape, scratch=(), prefetch=0):
    return pl.pallas_call(
        kernel,
        out_shape=out_shape,
        grid_spec=pltpu.PrefetchScalarGridSpec(
            num_scalar_prefetch=prefetch,
            grid=grid,
            in_specs=in_specs,
            out_specs=out_specs,
            scratch_shapes=scratch,
        ),
        compiler_params=pltpu.CompilerParams(
            dimension_semantics=("arbitrary",) * len(grid), vmem_limit_bytes=52 << 20
        ),
    )


def by_row(block, width):
    return pl.BlockSpec((block, width), lambda i, *_: (i, 0))


def whole(*shape):
    return pl.BlockSpec(shape, lambda i, *_: (0,) * len(shape))


def shaped(shape, dtype=jnp.bfloat16):
    return jax.ShapeDtypeStruct(shape, dtype)


def inverse_rms(values):
    return lax.rsqrt(jnp.mean(values * values, axis=-1, keepdims=True) + EPSILON)


def parts_in(parts, block):
    per = parts[0].shape[0] // block
    width = parts[0].shape[1]

    def spec(j):
        return pl.BlockSpec((block, width), lambda i, *_: (jnp.clip(i - j * per, 0, per - 1), 0))

    return [spec(j) for j in range(len(parts))]


def pick(refs, steps):
    value = refs[0][...]
    for j in range(1, len(refs)):
        value = jnp.where(pl.program_id(0) >= j * (steps // len(refs)), refs[j][...], value)
    return value


def halves(block, width, steps):
    per = steps // 2
    return [
        pl.BlockSpec((block, width), lambda i, *_: (jnp.minimum(i, per - 1), 0)),
        pl.BlockSpec((block, width), lambda i, *_: (jnp.maximum(i - per, 0), 0)),
    ]


def put(refs, value, steps):
    @pl.when(pl.program_id(0) < steps // 2)
    def _():
        refs[0][...] = value

    @pl.when(pl.program_id(0) >= steps // 2)
    def _():
        refs[1][...] = value


def eye(size):
    return low(
        wide32(lax.broadcasted_iota(jnp.int32, (size, size), 0) == lax.broadcasted_iota(jnp.int32, (size, size), 1))
    )


def pack_kernel(*refs):
    sources, (a_ref, b_ref), held, done = refs[:9], refs[9:11], refs[11:20], refs[20]
    copies = [pltpu.make_async_copy(src, dst, done.at[j]) for j, (src, dst) in enumerate(zip(sources, held))]
    for copy in copies:
        copy.start()
    for copy in copies:
        copy.wait()
    q_ref, k_ref, v_ref, o_ref, g1_ref, g2_ref, gate_ref, up_ref, down_ref = held
    rows, width = q_ref.shape
    hidden = gate_ref.shape[1]
    one = eye(rows)
    a_ref[:, :width] = q_ref[...]
    a_ref[:, width : 2 * width] = k_ref[...]
    a_ref[:, 2 * width : 3 * width] = v_ref[...]
    a_ref[:, 3 * width : 4 * width] = low(dot(one, o_ref[...], NT))
    line = lax.broadcasted_iota(jnp.int32, (a_ref.shape[1] - 4 * width, rows), 0)
    gains = jnp.where(line == 0, wide32(g1_ref[...]), jnp.where(line == 1, wide32(g2_ref[...]), 0.0))
    a_ref[:, 4 * width :] = low(dot(one, low(gains), NT))
    b_ref[:, :hidden] = gate_ref[...]
    b_ref[:, hidden : 2 * hidden] = up_ref[...]
    b_ref[:, 2 * hidden :] = down_ref[...]


def round_up(count):
    return -(-count // 128) * 128


def pack(q, k, v, o, gain_one, gain_two, gate, up, down):
    rows, width = q.shape
    first, second = round_up(4 * width + 2), 3 * gate.shape[1]
    if lax.axis_size("wide") != 8:
        a = jnp.concatenate([q, k, v, o.T, gain_one[:, None], gain_two[:, None]], axis=1)
        return jnp.pad(a, ((0, 0), (0, first - a.shape[1]))), jnp.concatenate([gate, up, down], axis=1)
    args = (q, k, v, o, gain_one[None], gain_two[None], gate, up, down)
    args = tuple(pltpu.with_memory_space_constraint(arg, pltpu.HBM) for arg in args)
    return call(
        pack_kernel,
        (1,),
        [pl.BlockSpec(memory_space=pltpu.HBM)] * len(args),
        [whole(rows, first), whole(rows, second)],
        [shaped((rows, first)), shaped((rows, second))],
        scratch=[pltpu.VMEM(arg.shape, arg.dtype) for arg in args] + [pltpu.SemaphoreType.DMA((len(args),))],
    )(*args)


def lay(place_ref, pieces, target):
    rows = pieces[0].shape[0]
    for j, piece in enumerate(pieces):
        target[pl.ds(pl.multiple_of(place_ref[j] * rows, 32), rows), :] = piece[...]


def project_kernel(place_ref, *refs, width, steps):
    xs, ws, (h_ref, q_ref, k_ref, v_ref, w_ref, out_ref, gain_ref) = refs[:4], refs[4:12], refs[12:]

    @pl.when(pl.program_id(0) == 0)
    def _():
        lay(place_ref, ws, w_ref)
        out_ref[...] = w_ref[:, 3 * width : 4 * width]
        gain_ref[...] = wide32(w_ref[:, 4 * width : 4 * width + 128]).T[:8]

    x = wide32(pick(xs, steps))
    h = low(x * inverse_rms(x) * gain_ref[0:1, :])
    h_ref[...] = h
    qkv = low(dot(h, w_ref[:, : 3 * width]))
    q_ref[...] = qkv[:, :width]
    k_ref[...] = qkv[:, width : 2 * width]
    v_ref[...] = qkv[:, 2 * width :]


def project(place, rows, pieces, width, block=512):
    d, full = rows[0].shape[1], pieces[0].shape[1]
    tokens = 4 * rows[0].shape[0]
    steps = tokens // block
    return call(
        functools.partial(project_kernel, width=width, steps=steps),
        (steps,),
        parts_in(rows, block) + [whole(*piece.shape) for piece in pieces],
        [by_row(block, d)] + [by_row(block, width)] * 3 + [whole(d, full), whole(d, width), whole(8, d)],
        [shaped((tokens, d))] + [shaped((tokens, width))] * 3 + [shaped((d, full)), shaped((d, width)), shaped((8, d), jnp.float32)],
        prefetch=1,
    )(place, *rows, *pieces)


def grads_kernel(place_ref, *refs, groups, steps, gain):
    if gain is not None:
        w_ref, gain_ref, norm_ref = refs[0], refs[1], refs[-2]
        refs = refs[2:-2] + refs[-1:]
    kept, (far, fourth), total = refs[-7:-3], refs[-3:-1], refs[-1]
    refs = list(refs[:-7])
    step = pl.program_id(0)

    def take(count):
        taken = refs[:count]
        del refs[:count]
        return pick(taken, steps)

    @pl.when(step == 0)
    def _():
        total[...] = jnp.zeros_like(total)

    at = 0
    for lhs_parts, rhs_parts in groups:
        lhs = take(lhs_parts)
        rhs = jnp.concatenate([take(count) for count in rhs_parts], axis=1)
        total[:, at : at + rhs.shape[1]] += dot(lhs, rhs, TN)
        at += rhs.shape[1]

    @pl.when(step == steps - 1)
    def _():
        rows = fourth.shape[0]

        def piece(j):
            return low(total[pl.ds(pl.multiple_of(place_ref[j] * rows, 32), rows), :])

        for j in range(4):
            kept[j][...] = piece(j)
        for j in range(3):
            far[j * rows : (j + 1) * rows, :] = piece(7 - j)
        fourth[...] = piece(4)
        if gain is not None:
            row, width = gain
            column = jnp.sum(wide32(w_ref[:, :width]) * total[:, :width], axis=1, keepdims=True)
            turned = jnp.broadcast_to(column, (column.shape[0], 128)).T
            norm_ref[...] = turned[:8] / gain_ref[row : row + 1, :]


def grad_pieces(place, groups, norm=None, block=512):
    arrays, counts, specs, full = [], [], [], 0
    if norm:
        arrays += norm[:2]
        specs += [whole(*array.shape) for array in norm[:2]]
    for lhs, rhs in groups:
        counts.append((len(lhs), [len(parts) for parts in rhs]))
        for parts in [lhs] + rhs:
            arrays += parts
            specs += parts_in(parts, block)
        full += sum(parts[0].shape[1] for parts in rhs)
    tokens = sum(part.shape[0] for part in groups[0][0])
    d = groups[0][0][0].shape[1]
    shapes = [(d // 8, full)] * 4 + [(3 * d // 8, full), (d // 8, full)]
    found = call(
        functools.partial(grads_kernel, groups=counts, steps=tokens // block, gain=norm[2:] if norm else None),
        (tokens // block,),
        specs,
        [whole(*shape) for shape in shapes] + [whole(8, d)] * bool(norm),
        [shaped(shape) for shape in shapes] + [shaped((8, d), jnp.float32)] * bool(norm),
        scratch=[pltpu.VMEM((d, full), jnp.float32)],
        prefetch=1,
    )(place, *arrays)
    return list(found[:4]), list(found[4:6]), *found[6:]


def finish_kernel(*refs, widths):
    pieces, outs = refs[: -len(widths)], refs[-len(widths) :]
    total = wide32(pieces[0][...])
    for piece in pieces[1:]:
        total = total + wide32(piece[...])
    at = 0
    for out, width in zip(outs, widths):
        part = total[:, at : at + width]
        out[...] = part.T if out.shape[1] == part.shape[0] else part
        at += width


def finish(pieces, widths, turned):
    if len(pieces) != 4:
        cuts = [sum(widths[: j + 1]) for j in range(len(widths) - 1)]
        parts = jnp.split(sum(wide32(piece) for piece in pieces), cuts, 1)
        return (*parts[:-1], parts[-1].T) if turned else parts
    rows, full = pieces[0].shape
    shapes = [(rows, width) for width in widths[:-1]] + [(widths[-1], rows) if turned else (rows, widths[-1])]
    return call(
        functools.partial(finish_kernel, widths=widths),
        (1,),
        [whole(rows, full)] * 4,
        [whole(*shape) for shape in shapes],
        [shaped(shape, jnp.float32) for shape in shapes],
    )(*pieces)


def key_bias(len_ref, cnt_ref, own_ref, row, items):
    unit = BUCKET // NARROW
    own = own_ref[0]
    col = lax.broadcasted_iota(jnp.int32, (1, BUCKET), 1)
    col = ((col // unit) ^ own) * unit + col % unit
    row = ((row // unit) ^ own) * unit
    start = jnp.int32(0)
    low_end = jnp.int32(0)
    high_end = jnp.int32(0)
    for i in range(items):
        length = len_ref[0, i]
        inside = (row >= start) & (row < start + length)
        low_end = jnp.where(inside, start, low_end)
        high_end = jnp.where(inside, start + cnt_ref[0, i], high_end)
        start = start + length
    return jnp.where((col >= low_end) & (col < high_end), 0.0, MASKED).astype(jnp.float32)


def forward_kernel(
    len_ref, cnt_ref, own_ref, q_ref, k_ref, v_ref, o_ref, lse_ref, *, first, block, heads, items
):
    bias = key_bias(len_ref, cnt_ref, own_ref, first + pl.program_id(0) * block, items)
    for h in range(heads):
        cols = slice(h * HEAD, (h + 1) * HEAD)
        scores = dot(q_ref[:, cols], k_ref[:, cols], NT) + bias
        highest = jnp.max(scores, axis=-1, keepdims=True)
        weights = jnp.exp(scores - highest)
        total = jnp.sum(weights, axis=-1, keepdims=True)
        o_ref[:, cols] = low(dot(low(weights), v_ref[:, cols]) / total)
        lse_ref[:, h : h + 1] = highest + jnp.log(total)


def attention_forward(scalars, q, k, v, first, block=256):
    tokens, width = q.shape
    heads, items = width // HEAD, scalars[0].shape[1]
    rows = tokens // 2
    at = first // block
    row = pl.BlockSpec((block, width), lambda i, *_: (i + at, 0))
    return call(
        functools.partial(forward_kernel, first=first, block=block, heads=heads, items=items),
        (rows // block,),
        [row, whole(tokens, width), whole(tokens, width)],
        [by_row(block, width), by_row(block, heads)],
        [shaped((rows, width)), shaped((rows, heads), jnp.float32)],
        prefetch=3,
    )(*scalars, q, k, v)


def backward_kernel(
    len_ref, cnt_ref, own_ref, q_ref, k_ref, v_ref, ga_ref, gb_ref, w_ref, o_ref, lse_ref, *rest, first, block, heads, items, steps
):
    if first:
        dk_in, dv_in, dq_ref, dk_ref, dv_ref, dk_sum, dv_sum = rest
    else:
        dq_ref, dk_sum, dv_sum = rest
    step = pl.program_id(0)
    bias = key_bias(len_ref, cnt_ref, own_ref, first + step * block, items)

    @pl.when(step == 0)
    def _():
        dk_sum[...] = dk_in[...] if first else jnp.zeros_like(dk_sum)
        dv_sum[...] = dv_in[...] if first else jnp.zeros_like(dv_sum)

    do_all = low(dot(pick((ga_ref, gb_ref), steps), w_ref[:, : heads * HEAD]))
    for h in range(heads):
        cols = slice(h * HEAD, (h + 1) * HEAD)
        q, k, v, do = q_ref[:, cols], k_ref[:, cols], v_ref[:, cols], do_all[:, cols]
        delta = jnp.sum(wide32(do) * wide32(o_ref[:, cols]), axis=-1, keepdims=True)
        probs = jnp.exp(dot(q, k, NT) + bias - lse_ref[:, h : h + 1])
        ds = low(probs * (dot(do, v, NT) - delta))
        dq_ref[:, cols] = low(dot(ds, k))
        dv_sum[cols, :] += dot(do, low(probs), TN)
        dk_sum[cols, :] += dot(q, ds, TN)

    if first:

        @pl.when(step == pl.num_programs(0) - 1)
        def _():
            dk_ref[...] = low(dk_sum[...].T)
            dv_ref[...] = low(dv_sum[...].T)


def attention_backward(scalars, q, k, v, grad, out_w, o, lse, sums, block=128):
    tokens, width = q.shape
    heads, items = width // HEAD, scalars[0].shape[1]
    rows = tokens // 2
    first = rows if sums else 0
    at = first // block
    row = pl.BlockSpec((block, width), lambda i, *_: (i + at, 0))
    full = whole(tokens, width)
    turned = whole(width, tokens)
    kept = shaped((width, tokens), jnp.float32)
    in_specs = [row, full, full] + parts_in(grad, block) + [whole(*out_w.shape), by_row(block, width), by_row(block, heads)]
    return call(
        functools.partial(backward_kernel, first=first, block=block, heads=heads, items=items, steps=rows // block),
        (rows // block,),
        in_specs + ([turned, turned] if sums else []),
        [by_row(block, width)] + ([full, full] if sums else [turned, turned]),
        [shaped((rows, width))] + ([shaped((tokens, width))] * 2 if sums else [kept, kept]),
        scratch=[pltpu.VMEM((width, tokens), jnp.float32)] * 2 if sums else [],
        prefetch=3,
    )(*scalars, q, k, v, *grad, out_w, o, lse, *sums)


def mlp_kernel(place_ref, *refs, width, heads_width, steps, near):
    xs, gs, os, ws, gain_ref = refs[:2], refs[2:4], refs[4:8], refs[8:12], refs[12]
    pieces, outs = (refs[13:14], refs[14:]) if near else (refs[13:21], refs[21:])
    ys, dhs, (h_ref, hid_ref, dg_ref, du_ref) = outs[:2], outs[2:4], outs[4:8]
    w_ref = pieces[0] if near else outs[8]
    if not near:

        @pl.when(pl.program_id(0) == 0)
        def _():
            lay(place_ref, pieces, w_ref)

    m = wide32(pick(xs, steps))
    for o_ref, out_ref in zip(os, ws):
        m = m + dot(o_ref[...], out_ref[:, :heads_width], NT)
    n = m * inverse_rms(m)
    h = low(n * gain_ref[1:2, :])
    h_ref[...] = h
    both = dot(h, w_ref[:, : 2 * width])
    gate, up = both[:, :width], both[:, width:]
    square = gate * gate
    scale = 0.7978845608028654
    t = jnp.tanh(scale * gate * (1.0 + 0.044715 * square))
    half = 0.5 * (1.0 + t)
    act = gate * half
    slope = half + (0.5 * scale) * gate * (1.0 - t * t) * (1.0 + 0.134145 * square)
    hid = low(act * up)
    hid_ref[...] = hid
    y = low(dot(hid, w_ref[:, 2 * width :], NT))
    dhid = dot(pick(gs, steps), w_ref[:, 2 * width :])
    dgate = low(dhid * up * slope)
    dup = low(dhid * act)
    dg_ref[...] = dgate
    du_ref[...] = dup
    dh = dot(dgate, w_ref[:, :width], NT) + dot(dup, w_ref[:, width : 2 * width], NT)
    put(ys, y, steps)
    put(dhs, low(dh), steps)
    if near:

        @pl.when(pl.program_id(0) < steps // 2)
        def _():
            outs[8][...] = m


def mlp(place, xs, gs, os, out_ws, gains, weight, near, block=256):
    part, d = xs[0].shape
    rows, steps = 2 * part, 2 * part // block
    width, heads_width = weight[0].shape[1] // 3, os[0].shape[1]
    wide_row, thin_row = by_row(block, d), by_row(block, width)
    split = halves(block, d, steps)
    other = pl.BlockSpec((block, heads_width), lambda i, *_: ((i + steps // 2) % steps, 0))
    out = call(
        functools.partial(mlp_kernel, width=width, heads_width=heads_width, steps=steps, near=near),
        (steps,),
        parts_in(xs, block) + parts_in(gs, block) + [by_row(block, heads_width), other] * 2
        + [whole(*out_ws[0].shape)] * 4 + [whole(8, d)] + [whole(*piece.shape) for piece in weight],
        split * 2 + [wide_row] + [thin_row] * 3 + (split[:1] if near else [whole(d, 3 * width)]),
        [shaped((part, d))] * 4 + [shaped((rows, d))] + [shaped((rows, width))] * 3
        + [shaped((part, d), jnp.float32) if near else shaped((d, 3 * width))],
        prefetch=1,
    )(place, *xs, *gs, *os, *out_ws, gains, *weight)
    return (out[:2], out[2:4]) + tuple(out[4:])


def rows_kernel(dq_ref, dk_ref, dv_ref, w_ref, dha_ref, dhb_ref, *, width, steps):
    dh = dot(dq_ref[...], w_ref[:, :width], NT)
    dh += dot(dk_ref[...], w_ref[:, width : 2 * width], NT)
    dh += dot(dv_ref[...], w_ref[:, 2 * width : 3 * width], NT)
    put((dha_ref, dhb_ref), low(dh), steps)


def rows_back(dq, dk, dv, weight, first, block=512):
    count, width = dq.shape
    d = weight.shape[0]
    at, steps = first // block, count // block
    late = pl.BlockSpec((block, width), lambda i, *_: (i + at, 0))
    return call(
        functools.partial(rows_kernel, width=width, steps=steps),
        (steps,),
        [by_row(block, width), late, late, whole(*weight.shape)],
        halves(block, d, steps),
        [shaped((count // 2, d))] * 2,
    )(dq, dk, dv, weight)


def norm_back(values, gain, grad):
    r = inverse_rms(values)
    n = values * r
    scaled = gain * grad
    return r * (scaled - n * jnp.mean(scaled * n, axis=-1, keepdims=True))


def on_device(
    patches, cotangent, item_len, valid_count, norm1_gain, query_weight, key_weight, value_weight,
    out_weight, norm2_gain, gate_weight, up_weight, down_weight,
):
    width = query_weight.shape[1]
    hidden = gate_weight.shape[1]
    scalars = (item_len, valid_count, lax.axis_index("narrow").astype(jnp.int32).reshape(1))
    place = places()
    attn_own, mlp_own = pack(
        query_weight, key_weight, value_weight, out_weight, norm1_gain, norm2_gain,
        gate_weight, up_weight, down_weight.T,
    )
    attn_pieces = gather_wide(attn_own)
    x = gather_rows(patches, attn_pieces[2:3])
    mlp_own = after(mlp_own, *attn_pieces[1:4])
    g = gather_rows(after(cotangent, *attn_pieces[1:4]))

    h_one, q, k, v, qkv_w, out_w, gains = project(place, x, attn_pieces, width)
    mlp_pieces = gather_wide(mlp_own, [gains])
    out_ws = gather_rows(after(out_w, g[2]))
    half = q.shape[0] // 2
    o_near, lse_near = attention_forward(scalars, q, k, v, 0)
    o_far_across = swap(o_near, "narrow", 2)
    o_far_across = (o_far_across, swap(o_far_across, "narrow", 1))
    o_far, lse_far = attention_forward(scalars, q, k, v, half)
    o_near_across = swap(o_far, "narrow", 2)
    o_far_all = (o_far, swap(o_far, "narrow", 1)) + o_far_across
    o_near_all = (o_near, swap(o_near, "narrow", 1), o_near_across, swap(o_near_across, "narrow", 1))
    y_far, dh_far, h2_far, hid_far, dg_far, du_far, mlp_w = mlp(
        place, x[2:], g[2:], o_far_all, out_ws, gains, mlp_pieces, False
    )
    from_far = cross(pair_sum(dh_far))
    y_near, dh_near, h2_near, hid_near, dg_near, du_near, middle_own = mlp(
        place, x[:2], g[:2], o_near_all, out_ws, gains, [mlp_w], True
    )
    gain_one, gain_two = gains[0:1], gains[1:2]
    dh_two = pair_sum(dh_near) + from_far
    mlp_kept, mlp_sent, norm_two = grad_pieces(
        place,
        [([h2_near, h2_far], [[dg_near, dg_far], [du_near, du_far]]), (list(g), [[hid_near, hid_far]])],
        [mlp_w, gains, 1, 2 * hidden],
    )
    mlp_sent = send_x(mlp_sent)
    middle_grad_own = wide32(cotangent) + norm_back(middle_own, gain_two, dh_two)
    d = gather_rows(low(middle_grad_own))
    mlp_pieces = reduce_wide([(mlp_kept, mlp_sent)])
    grad_gate, grad_up, grad_down = finish(mlp_pieces, (hidden, hidden, hidden), False)
    dq_near, dk_sum, dv_sum = attention_backward(scalars, q, k, v, d[:2], out_w, o_near, lse_near, ())
    output = low(middle_own + pair_sum(y_near) + cross(after(pair_sum(y_far), d[2])))
    out_kept, out_sent = grad_pieces(place, [(list(d), [[o_near, o_far]])])
    out_sent = send_x(out_sent)
    dq_far, dk, dv = attention_backward(scalars, q, k, v, d[2:], out_w, o_far, lse_far, (dk_sum, dv_sum))
    attn_kept, attn_sent, norm_one = grad_pieces(
        place, [([h_one], [[dq_near, dq_far], [dk], [dv]])], [qkv_w, gains, 0, 3 * width]
    )
    attn_sent = send_x(attn_sent)
    norms = sum_all(jnp.concatenate([norm_one[:1], norm_two[:1]], axis=0))
    dh_far = rows_back(dq_far, dk, dv, qkv_w, half)
    from_far = cross(pair_sum(dh_far))
    dh_near = rows_back(dq_near, dk, dv, qkv_w, 0)
    grad_query, grad_key, grad_value, grad_out = finish(
        reduce_wide([(attn_kept, attn_sent), (out_kept, out_sent)]), (width, width, width, width), True
    )
    dh_one = pair_sum(dh_near) + from_far
    grad_input = middle_grad_own + norm_back(wide32(patches), gain_one, dh_one)
    return (
        output, grad_input, norms[0], grad_query, grad_key, grad_value, grad_out, norms[1],
        grad_gate, grad_up, grad_down.T,
    )


def solution(mesh):
    tokens = P(("wide", "narrow"), None)

    return jax.shard_map(
        on_device,
        mesh=mesh,
        in_specs=(
            tokens, tokens, P("wide", None), P("wide", None), P("wide"), P("wide", "narrow"),
            P("wide", "narrow"), P("wide", "narrow"), P("narrow", "wide"), P("wide"),
            P("wide", "narrow"), P("wide", "narrow"), P("narrow", "wide"),
        ),
        out_specs=(
            tokens, tokens, P("wide"), P("wide", "narrow"), P("wide", "narrow"), P("wide", "narrow"),
            P("narrow", "wide"), P("wide"), P("wide", "narrow"), P("wide", "narrow"), P("narrow", "wide"),
        ),
        check_vma=False,
    )
```

```python
import functools

import jax
import jax.numpy as jnp
from jax import lax
from jax.experimental import pallas as pl
from jax.experimental.pallas import tpu as pltpu
from jax.sharding import PartitionSpec as P

HEAD = 64
BUCKET = 2048
EPSILON = 1e-06
MASKED = -1e30
NARROW = 4
WIDE = "wide"
ACROSS = "narrow"


NT = (((1,), (1,)), ((), ()))
NN = (((1,), (0,)), ((), ()))
TN = (((0,), (0,)), ((), ()))


def dot(left, right, dims=NN):
    return lax.dot_general(left, right, dims, preferred_element_type=jnp.float32)


def low(values):
    return values.astype(jnp.bfloat16)


def wide32(values):
    return values.astype(jnp.float32)


def swap(values, axis, bits):
    size = lax.axis_size(axis)
    return lax.ppermute(values, axis, [(i, i ^ bits) for i in range(size)])


def after(values, *earlier):
    return lax.optimization_barrier((values, *earlier))[0]


def gather_rows(own, ready=()):
    across = swap(own, ACROSS, 2)
    near, far = after(own, *ready), after(across, *ready)
    return own, swap(near, ACROSS, 1), across, swap(far, ACROSS, 1)


def pair_sum(parts):
    return wide32(parts[0]) + wide32(swap(parts[1], ACROSS, 1))


def cross(values):
    return wide32(swap(low(values), ACROSS, 2))


def places():
    if lax.axis_size(WIDE) != 8:
        return jnp.arange(8, dtype=jnp.int32)
    index = lax.axis_index(WIDE).astype(jnp.int32)
    order = jnp.array([0, 2, 4, 6, 1, 3, 5, 7], jnp.int32)
    return jnp.bitwise_xor(order, index)


def gather_wide(own, ready=()):
    if lax.axis_size(WIDE) != 8:
        return jnp.split(lax.all_gather(own, WIDE, axis=0, tiled=True), 8, axis=0)
    column = [own] + [swap(own, WIDE, 2 * k) for k in (1, 2, 3)]
    sent = [after(own, *ready)] + column[1:]
    return column + [swap(piece, WIDE, 1) for piece in sent]


def send_x(sent):
    if lax.axis_size(WIDE) != 8:
        return sent
    return [swap(part, WIDE, 1) for part in sent]


def add_x(kept, received):
    rows = kept[0].shape[0]
    far = [received[0][j * rows : (j + 1) * rows] for j in range(3)]
    added = [low(wide32(mine) + wide32(other)) for mine, other in zip(kept[1:], far[::-1])]
    return [low(wide32(kept[0]) + wide32(received[1]))] + added


def send_z(column):
    return [column[0]] + [swap(column[k], WIDE, 2 * k) for k in (3, 2, 1)]


def reduce_wide(parts):
    size = lax.axis_size(WIDE)
    if size == 8:
        columns = [add_x(kept, received) for kept, received in parts]
        return send_z([jnp.concatenate(pieces, axis=1) for pieces in zip(*columns)])
    full = []
    for kept, sent in parts:
        rows = kept[0].shape[0]
        far = [sent[0][j * rows : (j + 1) * rows] for j in range(3)]
        full.append(jnp.concatenate(kept + [sent[1]] + far[::-1], axis=0))
    full = jnp.concatenate(full, axis=1)
    return list(lax.all_to_all(full.reshape(size, -1, full.shape[1]), WIDE, 0, 0, tiled=True))


def sum_all(values):
    size = lax.axis_size(WIDE)
    if size != 8:
        values = lax.psum(values, WIDE)
    else:
        for bits in (2, 4, 1):
            values = values + swap(values, WIDE, bits)
    values = values + swap(values, ACROSS, 2)
    values = values + swap(values, ACROSS, 1)
    rows = values.shape[1] // size
    return lax.dynamic_slice_in_dim(values, lax.axis_index(WIDE) * rows, rows, 1)


def call(kernel, grid, in_specs, out_specs, out_shape, scratch=(), prefetch=0):
    return pl.pallas_call(
        kernel,
        out_shape=out_shape,
        grid_spec=pltpu.PrefetchScalarGridSpec(
            num_scalar_prefetch=prefetch,
            grid=grid,
            in_specs=in_specs,
            out_specs=out_specs,
            scratch_shapes=scratch,
        ),
        compiler_params=pltpu.CompilerParams(
            dimension_semantics=("arbitrary",) * len(grid), vmem_limit_bytes=52 << 20
        ),
    )


def by_row(block, width):
    return pl.BlockSpec((block, width), lambda i, *_: (i, 0))


def whole(*shape):
    return pl.BlockSpec(shape, lambda i, *_: (0,) * len(shape))


def shaped(shape, dtype=jnp.bfloat16):
    return jax.ShapeDtypeStruct(shape, dtype)


def inverse_rms(values):
    return lax.rsqrt(jnp.mean(values * values, axis=-1, keepdims=True) + EPSILON)


def parts_in(parts, block):
    per = parts[0].shape[0] // block
    width = parts[0].shape[1]

    def spec(j):
        return pl.BlockSpec((block, width), lambda i, *_: (jnp.clip(i - j * per, 0, per - 1), 0))

    return [spec(j) for j in range(len(parts))]


def pick(refs, steps):
    value = refs[0][...]
    for j in range(1, len(refs)):
        value = jnp.where(pl.program_id(0) >= j * (steps // len(refs)), refs[j][...], value)
    return value


def halves(block, width, steps):
    per = steps // 2
    return [
        pl.BlockSpec((block, width), lambda i, *_: (jnp.minimum(i, per - 1), 0)),
        pl.BlockSpec((block, width), lambda i, *_: (jnp.maximum(i - per, 0), 0)),
    ]


def put(refs, value, steps):
    @pl.when(pl.program_id(0) < steps // 2)
    def _():
        refs[0][...] = value

    @pl.when(pl.program_id(0) >= steps // 2)
    def _():
        refs[1][...] = value


def eye(size):
    return low(
        wide32(lax.broadcasted_iota(jnp.int32, (size, size), 0) == lax.broadcasted_iota(jnp.int32, (size, size), 1))
    )


def pack_kernel(*refs):
    sources, (a_ref, b_ref), held, done = refs[:9], refs[9:11], refs[11:20], refs[20]
    copies = [pltpu.make_async_copy(src, dst, done.at[j]) for j, (src, dst) in enumerate(zip(sources, held))]
    for copy in copies:
        copy.start()
    for copy in copies:
        copy.wait()
    q_ref, k_ref, v_ref, o_ref, g1_ref, g2_ref, gate_ref, up_ref, down_ref = held
    rows, width = q_ref.shape
    hidden = gate_ref.shape[1]
    one = eye(rows)
    a_ref[:, :width] = q_ref[...]
    a_ref[:, width : 2 * width] = k_ref[...]
    a_ref[:, 2 * width : 3 * width] = v_ref[...]
    a_ref[:, 3 * width : 4 * width] = low(dot(one, o_ref[...], NT))
    line = lax.broadcasted_iota(jnp.int32, (a_ref.shape[1] - 4 * width, rows), 0)
    gains = jnp.where(line == 0, wide32(g1_ref[...]), jnp.where(line == 1, wide32(g2_ref[...]), 0.0))
    a_ref[:, 4 * width :] = low(dot(one, low(gains), NT))
    b_ref[:, :hidden] = gate_ref[...]
    b_ref[:, hidden : 2 * hidden] = up_ref[...]
    b_ref[:, 2 * hidden :] = down_ref[...]


def round_up(count):
    return -(-count // 128) * 128


def pack(q, k, v, o, gain_one, gain_two, gate, up, down):
    rows, width = q.shape
    first, second = round_up(4 * width + 2), 3 * gate.shape[1]
    if lax.axis_size(WIDE) != 8:
        a = jnp.concatenate([q, k, v, o.T, gain_one[:, None], gain_two[:, None]], axis=1)
        return jnp.pad(a, ((0, 0), (0, first - a.shape[1]))), jnp.concatenate([gate, up, down], axis=1)
    args = (q, k, v, o, gain_one[None], gain_two[None], gate, up, down)
    args = tuple(pltpu.with_memory_space_constraint(arg, pltpu.HBM) for arg in args)
    return call(
        pack_kernel,
        (1,),
        [pl.BlockSpec(memory_space=pltpu.HBM)] * len(args),
        [whole(rows, first), whole(rows, second)],
        [shaped((rows, first)), shaped((rows, second))],
        scratch=[pltpu.VMEM(arg.shape, arg.dtype) for arg in args] + [pltpu.SemaphoreType.DMA((len(args),))],
    )(*args)


def lay(place_ref, pieces, target):
    rows = pieces[0].shape[0]
    for j, piece in enumerate(pieces):
        target[pl.ds(pl.multiple_of(place_ref[j] * rows, 32), rows), :] = piece[...]


def project_kernel(place_ref, *refs, width, steps):
    xs, ws, (h_ref, q_ref, k_ref, v_ref, w_ref, out_ref, gain_ref) = refs[:4], refs[4:12], refs[12:]

    @pl.when(pl.program_id(0) == 0)
    def _():
        lay(place_ref, ws, w_ref)
        out_ref[...] = w_ref[:, 3 * width : 4 * width]
        gain_ref[...] = wide32(w_ref[:, 4 * width : 4 * width + 128]).T[:8]

    x = wide32(pick(xs, steps))
    h = low(x * inverse_rms(x) * gain_ref[0:1, :])
    h_ref[...] = h
    qkv = low(dot(h, w_ref[:, : 3 * width]))
    q_ref[...] = qkv[:, :width]
    k_ref[...] = qkv[:, width : 2 * width]
    v_ref[...] = qkv[:, 2 * width :]


def project(place, rows, pieces, width, block=512):
    d, full = rows[0].shape[1], pieces[0].shape[1]
    tokens = 4 * rows[0].shape[0]
    steps = tokens // block
    return call(
        functools.partial(project_kernel, width=width, steps=steps),
        (steps,),
        parts_in(rows, block) + [whole(*piece.shape) for piece in pieces],
        [by_row(block, d)] + [by_row(block, width)] * 3 + [whole(d, full), whole(d, width), whole(8, d)],
        [shaped((tokens, d))] + [shaped((tokens, width))] * 3 + [shaped((d, full)), shaped((d, width)), shaped((8, d), jnp.float32)],
        prefetch=1,
    )(place, *rows, *pieces)


def grads_kernel(place_ref, *refs, groups, steps, gain):
    if gain is not None:
        w_ref, gain_ref, norm_ref = refs[0], refs[1], refs[-2]
        refs = refs[2:-2] + refs[-1:]
    kept, (far, fourth), total = refs[-7:-3], refs[-3:-1], refs[-1]
    refs = list(refs[:-7])
    step = pl.program_id(0)

    def take(count):
        taken = refs[:count]
        del refs[:count]
        return pick(taken, steps)

    @pl.when(step == 0)
    def _():
        total[...] = jnp.zeros_like(total)

    at = 0
    for lhs_parts, rhs_parts in groups:
        lhs = take(lhs_parts)
        rhs = jnp.concatenate([take(count) for count in rhs_parts], axis=1)
        total[:, at : at + rhs.shape[1]] += dot(lhs, rhs, TN)
        at += rhs.shape[1]

    @pl.when(step == steps - 1)
    def _():
        rows = fourth.shape[0]

        def piece(j):
            return low(total[pl.ds(pl.multiple_of(place_ref[j] * rows, 32), rows), :])

        for j in range(4):
            kept[j][...] = piece(j)
        for j in range(3):
            far[j * rows : (j + 1) * rows, :] = piece(7 - j)
        fourth[...] = piece(4)
        if gain is not None:
            row, width = gain
            column = jnp.sum(wide32(w_ref[:, :width]) * total[:, :width], axis=1, keepdims=True)
            turned = jnp.broadcast_to(column, (column.shape[0], 128)).T
            norm_ref[...] = turned[:8] / gain_ref[row : row + 1, :]


def grad_pieces(place, groups, norm=None, block=512):
    arrays, counts, specs, full = [], [], [], 0
    if norm:
        arrays += norm[:2]
        specs += [whole(*array.shape) for array in norm[:2]]
    for lhs, rhs in groups:
        counts.append((len(lhs), [len(parts) for parts in rhs]))
        for parts in [lhs] + rhs:
            arrays += parts
            specs += parts_in(parts, block)
        full += sum(parts[0].shape[1] for parts in rhs)
    tokens = sum(part.shape[0] for part in groups[0][0])
    d = groups[0][0][0].shape[1]
    shapes = [(d // 8, full)] * 4 + [(3 * d // 8, full), (d // 8, full)]
    found = call(
        functools.partial(grads_kernel, groups=counts, steps=tokens // block, gain=norm[2:] if norm else None),
        (tokens // block,),
        specs,
        [whole(*shape) for shape in shapes] + [whole(8, d)] * bool(norm),
        [shaped(shape) for shape in shapes] + [shaped((8, d), jnp.float32)] * bool(norm),
        scratch=[pltpu.VMEM((d, full), jnp.float32)],
        prefetch=1,
    )(place, *arrays)
    return list(found[:4]), list(found[4:6]), *found[6:]


def finish_kernel(*refs, widths):
    pieces, outs = refs[: -len(widths)], refs[-len(widths) :]
    total = wide32(pieces[0][...])
    for piece in pieces[1:]:
        total = total + wide32(piece[...])
    at = 0
    for out, width in zip(outs, widths):
        part = total[:, at : at + width]
        out[...] = part.T if out.shape[1] == part.shape[0] else part
        at += width


def finish(pieces, widths, turned):
    if len(pieces) != 4:
        cuts = [sum(widths[: j + 1]) for j in range(len(widths) - 1)]
        parts = jnp.split(sum(wide32(piece) for piece in pieces), cuts, 1)
        return (*parts[:-1], parts[-1].T) if turned else parts
    rows, full = pieces[0].shape
    shapes = [(rows, width) for width in widths[:-1]] + [(widths[-1], rows) if turned else (rows, widths[-1])]
    return call(
        functools.partial(finish_kernel, widths=widths),
        (1,),
        [whole(rows, full)] * 4,
        [whole(*shape) for shape in shapes],
        [shaped(shape, jnp.float32) for shape in shapes],
    )(*pieces)


def key_bias(len_ref, cnt_ref, own_ref, row, items):
    unit = BUCKET // NARROW
    own = own_ref[0]
    col = lax.broadcasted_iota(jnp.int32, (1, BUCKET), 1)
    col = ((col // unit) ^ own) * unit + col % unit
    row = ((row // unit) ^ own) * unit
    start = jnp.int32(0)
    low_end = jnp.int32(0)
    high_end = jnp.int32(0)
    for i in range(items):
        length = len_ref[0, i]
        inside = (row >= start) & (row < start + length)
        low_end = jnp.where(inside, start, low_end)
        high_end = jnp.where(inside, start + cnt_ref[0, i], high_end)
        start = start + length
    return jnp.where((col >= low_end) & (col < high_end), 0.0, MASKED).astype(jnp.float32)


def forward_kernel(
    len_ref, cnt_ref, own_ref, q_ref, k_ref, v_ref, o_ref, lse_ref, *, first, block, heads, items
):
    bias = key_bias(len_ref, cnt_ref, own_ref, first + pl.program_id(0) * block, items)
    for h in range(heads):
        cols = slice(h * HEAD, (h + 1) * HEAD)
        scores = dot(q_ref[:, cols], k_ref[:, cols], NT) + bias
        highest = jnp.max(scores, axis=-1, keepdims=True)
        weights = jnp.exp(scores - highest)
        total = jnp.sum(weights, axis=-1, keepdims=True)
        o_ref[:, cols] = low(dot(low(weights), v_ref[:, cols]) / total)
        lse_ref[:, h : h + 1] = highest + jnp.log(total)


def attention_forward(scalars, q, k, v, first, block=256):
    tokens, width = q.shape
    heads, items = width // HEAD, scalars[0].shape[1]
    rows = tokens // 2
    at = first // block
    row = pl.BlockSpec((block, width), lambda i, *_: (i + at, 0))
    return call(
        functools.partial(forward_kernel, first=first, block=block, heads=heads, items=items),
        (rows // block,),
        [row, whole(tokens, width), whole(tokens, width)],
        [by_row(block, width), by_row(block, heads)],
        [shaped((rows, width)), shaped((rows, heads), jnp.float32)],
        prefetch=3,
    )(*scalars, q, k, v)


def backward_kernel(
    len_ref, cnt_ref, own_ref, q_ref, k_ref, v_ref, ga_ref, gb_ref, w_ref, o_ref, lse_ref, *rest, first, block, heads, items, steps
):
    if first:
        dk_in, dv_in, dq_ref, dk_ref, dv_ref, dk_sum, dv_sum = rest
    else:
        dq_ref, dk_sum, dv_sum = rest
    step = pl.program_id(0)
    bias = key_bias(len_ref, cnt_ref, own_ref, first + step * block, items)

    @pl.when(step == 0)
    def _():
        dk_sum[...] = dk_in[...] if first else jnp.zeros_like(dk_sum)
        dv_sum[...] = dv_in[...] if first else jnp.zeros_like(dv_sum)

    do_all = low(dot(pick((ga_ref, gb_ref), steps), w_ref[:, : heads * HEAD]))
    for h in range(heads):
        cols = slice(h * HEAD, (h + 1) * HEAD)
        q, k, v, do = q_ref[:, cols], k_ref[:, cols], v_ref[:, cols], do_all[:, cols]
        delta = jnp.sum(wide32(do) * wide32(o_ref[:, cols]), axis=-1, keepdims=True)
        probs = jnp.exp(dot(q, k, NT) + bias - lse_ref[:, h : h + 1])
        ds = low(probs * (dot(do, v, NT) - delta))
        dq_ref[:, cols] = low(dot(ds, k))
        dv_sum[cols, :] += dot(do, low(probs), TN)
        dk_sum[cols, :] += dot(q, ds, TN)

    if first:

        @pl.when(step == pl.num_programs(0) - 1)
        def _():
            dk_ref[...] = low(dk_sum[...].T)
            dv_ref[...] = low(dv_sum[...].T)


def attention_backward(scalars, q, k, v, grad, out_w, o, lse, sums, block=128):
    tokens, width = q.shape
    heads, items = width // HEAD, scalars[0].shape[1]
    rows = tokens // 2
    first = rows if sums else 0
    at = first // block
    row = pl.BlockSpec((block, width), lambda i, *_: (i + at, 0))
    full = whole(tokens, width)
    turned = whole(width, tokens)
    kept = shaped((width, tokens), jnp.float32)
    in_specs = [row, full, full] + parts_in(grad, block) + [whole(*out_w.shape), by_row(block, width), by_row(block, heads)]
    return call(
        functools.partial(backward_kernel, first=first, block=block, heads=heads, items=items, steps=rows // block),
        (rows // block,),
        in_specs + ([turned, turned] if sums else []),
        [by_row(block, width)] + ([full, full] if sums else [turned, turned]),
        [shaped((rows, width))] + ([shaped((tokens, width))] * 2 if sums else [kept, kept]),
        scratch=[pltpu.VMEM((width, tokens), jnp.float32)] * 2 if sums else [],
        prefetch=3,
    )(*scalars, q, k, v, *grad, out_w, o, lse, *sums)


def mlp_kernel(place_ref, *refs, width, heads_width, steps, near):
    xs, gs, os, ws, gain_ref = refs[:2], refs[2:4], refs[4:8], refs[8:12], refs[12]
    pieces, outs = (refs[13:14], refs[14:]) if near else (refs[13:21], refs[21:])
    ys, dhs, (h_ref, hid_ref, dg_ref, du_ref) = outs[:2], outs[2:4], outs[4:8]
    w_ref = pieces[0] if near else outs[8]
    if not near:

        @pl.when(pl.program_id(0) == 0)
        def _():
            lay(place_ref, pieces, w_ref)

    m = wide32(pick(xs, steps))
    for o_ref, out_ref in zip(os, ws):
        m = m + dot(o_ref[...], out_ref[:, :heads_width], NT)
    n = m * inverse_rms(m)
    h = low(n * gain_ref[1:2, :])
    h_ref[...] = h
    both = dot(h, w_ref[:, : 2 * width])
    gate, up = both[:, :width], both[:, width:]
    square = gate * gate
    scale = 0.7978845608028654
    t = jnp.tanh(scale * gate * (1.0 + 0.044715 * square))
    half = 0.5 * (1.0 + t)
    act = gate * half
    slope = half + (0.5 * scale) * gate * (1.0 - t * t) * (1.0 + 0.134145 * square)
    hid = low(act * up)
    hid_ref[...] = hid
    y = low(dot(hid, w_ref[:, 2 * width :], NT))
    dhid = dot(pick(gs, steps), w_ref[:, 2 * width :])
    dgate = low(dhid * up * slope)
    dup = low(dhid * act)
    dg_ref[...] = dgate
    du_ref[...] = dup
    dh = dot(dgate, w_ref[:, :width], NT) + dot(dup, w_ref[:, width : 2 * width], NT)
    put(ys, y, steps)
    put(dhs, low(dh), steps)
    if near:

        @pl.when(pl.program_id(0) < steps // 2)
        def _():
            outs[8][...] = m


def mlp(place, xs, gs, os, out_ws, gains, weight, near, block=256):
    part, d = xs[0].shape
    rows, steps = 2 * part, 2 * part // block
    width, heads_width = weight[0].shape[1] // 3, os[0].shape[1]
    wide_row, thin_row = by_row(block, d), by_row(block, width)
    split = halves(block, d, steps)
    other = pl.BlockSpec((block, heads_width), lambda i, *_: ((i + steps // 2) % steps, 0))
    out = call(
        functools.partial(mlp_kernel, width=width, heads_width=heads_width, steps=steps, near=near),
        (steps,),
        parts_in(xs, block) + parts_in(gs, block) + [by_row(block, heads_width), other] * 2
        + [whole(*out_ws[0].shape)] * 4 + [whole(8, d)] + [whole(*piece.shape) for piece in weight],
        split * 2 + [wide_row] + [thin_row] * 3 + (split[:1] if near else [whole(d, 3 * width)]),
        [shaped((part, d))] * 4 + [shaped((rows, d))] + [shaped((rows, width))] * 3
        + [shaped((part, d), jnp.float32) if near else shaped((d, 3 * width))],
        prefetch=1,
    )(place, *xs, *gs, *os, *out_ws, gains, *weight)
    return (out[:2], out[2:4]) + tuple(out[4:])


def rows_kernel(dq_ref, dk_ref, dv_ref, w_ref, dha_ref, dhb_ref, *, width, steps):
    dh = dot(dq_ref[...], w_ref[:, :width], NT)
    dh += dot(dk_ref[...], w_ref[:, width : 2 * width], NT)
    dh += dot(dv_ref[...], w_ref[:, 2 * width : 3 * width], NT)
    put((dha_ref, dhb_ref), low(dh), steps)


def rows_back(dq, dk, dv, weight, first, block=512):
    count, width = dq.shape
    d = weight.shape[0]
    at, steps = first // block, count // block
    late = pl.BlockSpec((block, width), lambda i, *_: (i + at, 0))
    return call(
        functools.partial(rows_kernel, width=width, steps=steps),
        (steps,),
        [by_row(block, width), late, late, whole(*weight.shape)],
        halves(block, d, steps),
        [shaped((count // 2, d))] * 2,
    )(dq, dk, dv, weight)


def norm_back(values, gain, grad):
    r = inverse_rms(values)
    n = values * r
    scaled = gain * grad
    return r * (scaled - n * jnp.mean(scaled * n, axis=-1, keepdims=True))


def on_device(
    patches, cotangent, item_len, valid_count, norm1_gain, query_weight, key_weight, value_weight,
    out_weight, norm2_gain, gate_weight, up_weight, down_weight,
):
    width = query_weight.shape[1]
    hidden = gate_weight.shape[1]
    scalars = (item_len, valid_count, lax.axis_index(ACROSS).astype(jnp.int32).reshape(1))
    place = places()
    attn_own, mlp_own = pack(
        query_weight, key_weight, value_weight, out_weight, norm1_gain, norm2_gain,
        gate_weight, up_weight, down_weight.T,
    )
    attn_pieces = gather_wide(attn_own)
    x = gather_rows(patches, attn_pieces[2:3])
    mlp_own = after(mlp_own, *attn_pieces[1:4])
    g = gather_rows(after(cotangent, *attn_pieces[1:4]))

    h_one, q, k, v, qkv_w, out_w, gains = project(place, x, attn_pieces, width)
    mlp_pieces = gather_wide(mlp_own, [gains])
    out_ws = gather_rows(after(out_w, g[2]))
    half = q.shape[0] // 2
    o_near, lse_near = attention_forward(scalars, q, k, v, 0)
    o_far_across = swap(o_near, ACROSS, 2)
    o_far_across = (o_far_across, swap(o_far_across, ACROSS, 1))
    o_far, lse_far = attention_forward(scalars, q, k, v, half)
    o_near_across = swap(o_far, ACROSS, 2)
    o_far_all = (o_far, swap(o_far, ACROSS, 1)) + o_far_across
    o_near_all = (o_near, swap(o_near, ACROSS, 1), o_near_across, swap(o_near_across, ACROSS, 1))
    y_far, dh_far, h2_far, hid_far, dg_far, du_far, mlp_w = mlp(
        place, x[2:], g[2:], o_far_all, out_ws, gains, mlp_pieces, False
    )
    from_far = cross(pair_sum(dh_far))
    y_near, dh_near, h2_near, hid_near, dg_near, du_near, middle_own = mlp(
        place, x[:2], g[:2], o_near_all, out_ws, gains, [mlp_w], True
    )
    gain_one, gain_two = gains[0:1], gains[1:2]
    dh_two = pair_sum(dh_near) + from_far
    mlp_kept, mlp_sent, norm_two = grad_pieces(
        place,
        [([h2_near, h2_far], [[dg_near, dg_far], [du_near, du_far]]), (list(g), [[hid_near, hid_far]])],
        [mlp_w, gains, 1, 2 * hidden],
    )
    mlp_sent = send_x(mlp_sent)
    middle_grad_own = wide32(cotangent) + norm_back(middle_own, gain_two, dh_two)
    d = gather_rows(low(middle_grad_own))
    mlp_pieces = reduce_wide([(mlp_kept, mlp_sent)])
    grad_gate, grad_up, grad_down = finish(mlp_pieces, (hidden, hidden, hidden), False)
    dq_near, dk_sum, dv_sum = attention_backward(scalars, q, k, v, d[:2], out_w, o_near, lse_near, ())
    y_from_far = cross(after(pair_sum(y_far), d[2]))
    out_kept, out_sent = grad_pieces(place, [(list(d), [[o_near, o_far]])])
    out_sent = send_x(out_sent)
    dq_far, dk, dv = attention_backward(scalars, q, k, v, d[2:], out_w, o_far, lse_far, (dk_sum, dv_sum))
    attn_kept, attn_sent, norm_one = grad_pieces(
        place, [([h_one], [[dq_near, dq_far], [dk], [dv]])], [qkv_w, gains, 0, 3 * width]
    )
    attn_sent = send_x(attn_sent)
    norms = sum_all(jnp.concatenate([norm_one[:1], norm_two[:1]], axis=0))
    dh_far = rows_back(dq_far, dk, dv, qkv_w, half)
    from_far = cross(pair_sum(dh_far))
    dh_near = rows_back(dq_near, dk, dv, qkv_w, 0)
    grad_query, grad_key, grad_value, grad_out = finish(
        reduce_wide([(attn_kept, attn_sent), (out_kept, out_sent)]), (width, width, width, width), True
    )
    dh_one = pair_sum(dh_near) + from_far
    y_own = pair_sum((y_near[0], after(y_near[1], dh_near[0])))
    output = low(middle_own + y_own + y_from_far)
    grad_input = middle_grad_own + norm_back(wide32(patches), gain_one, dh_one)
    return (
        output, grad_input, norms[0], grad_query, grad_key, grad_value, grad_out, norms[1],
        grad_gate, grad_up, grad_down.T,
    )


def solution(mesh):
    tokens = P((WIDE, ACROSS), None)

    return jax.shard_map(
        on_device,
        mesh=mesh,
        in_specs=(
            tokens, tokens, P(WIDE, None), P(WIDE, None), P(WIDE), P(WIDE, ACROSS),
            P(WIDE, ACROSS), P(WIDE, ACROSS), P(ACROSS, WIDE), P(WIDE),
            P(WIDE, ACROSS), P(WIDE, ACROSS), P(ACROSS, WIDE),
        ),
        out_specs=(
            tokens, tokens, P(WIDE), P(WIDE, ACROSS), P(WIDE, ACROSS), P(WIDE, ACROSS),
            P(ACROSS, WIDE), P(WIDE), P(WIDE, ACROSS), P(WIDE, ACROSS), P(ACROSS, WIDE),
        ),
        check_vma=False,
    )
```
